512 devices in a mesh: fsdp: 8 (over y, x_lo), tensor: 64 (over x_hi, z, core).
Axes of the slice: x: 4 (x_hi: 2, x_lo: 2; x = x_hi * 2 + x_lo), y: 4, z: 16, core: 2. Of those that a mesh axis runs over, the one named last changes fastest.
Arguments:
- tokens: bfloat16 [1024, 8192], P('fsdp', 'tensor'), may hold values from -6 to 6
- in_values: bfloat16 [8192, 3, 8192], P('fsdp', None, 'tensor'), may hold values from -0.1875 to 0.1875
- in_scales: bfloat16 [64, 3, 8192], P('fsdp', None, 'tensor'), may hold values from 0.5 to 2
- filters: float32 [512, 128], P('tensor'), may hold values from -0.6 to 0.6
- out_weight: bfloat16 [8192, 8192], P('tensor', 'fsdp'), may hold values from -0.0625 to 0.0625
- cotangent: bfloat16 [1024, 8192], P('fsdp', 'tensor'), may hold values from -15 to 15
Outputs:
- input_grad: bfloat16 [1024, 8192], P('fsdp', 'tensor')
- filter_grad: float32 [512, 128], P('tensor')
The draws below stay inside these ranges and needn't reach their ends.
All inputs are finite; a program needn't handle non-finite values.
Results may differ from the reference program's by a relative error of at most 0.012.
Values may be sent and summed in bfloat16 or wider, within the bound.
A program may use at most 128 MiB of HBM per device.

```python
import math
import jax
import jax.numpy as jnp
from jax import lax

D = 8192
GROUP = 16
TAPS = 128
BLOCK = 128
TOK_DEV = 128
LENGTH = 1024


def draw_filters(key, part):
    key_noise = jax.random.fold_in(key, 11)
    key_rate = jax.random.fold_in(key, 23)
    lags = jnp.arange(TAPS, dtype=jnp.float32)[None, :]
    noise = jnp.clip(jax.random.normal(key_noise, (D // GROUP, TAPS), jnp.float32), -4.0, 4.0)
    rates = jnp.exp(jax.random.uniform(key_rate, (D // GROUP, 1), jnp.float32, math.log(1.0 / 400.0), math.log(1.0 / 25.0)))
    return 0.15 * noise * jnp.exp(-rates * lags)


def draw_cotangent(key, part):
    key_noise = jax.random.fold_in(key, 37)
    ramp = 1.0 + 2.0 * jnp.arange(LENGTH, dtype=jnp.float32)[:, None] / (LENGTH - 1)
    noise = jnp.clip(jax.random.normal(key_noise, (LENGTH, D), jnp.float32), -5.0, 5.0)
    return (noise * ramp).astype(jnp.bfloat16)


def strengthened(result, key, source, target, shards_of, factor):
    owner, partner = [(jnp.arange(result.shape[position]) // (result.shape[position] // shards_of)).reshape([-1 if axis == position else 1 for axis in range(result.ndim)]) for position in (source, target)]
    chosen = jax.random.permutation(key, shards_of)[partner]
    strong = (owner == chosen) | (owner == (partner + shards_of // 2) % shards_of)
    return jnp.where(strong, factor * result, result)


def levels(rng, shape, cuts, smallest, largest):
    loudness = 1.0
    for axis_at, parts in cuts:
        steps = jax.random.uniform(jax.random.fold_in(jax.random.fold_in(rng, 6), axis_at), (parts,), jnp.float32, smallest / len(cuts), largest / len(cuts))
        loudness = loudness * jnp.repeat(jnp.exp(steps), shape[axis_at] // parts).reshape((-1,) + (1,) * (len(shape) - 1 - axis_at))
    return loudness


def normal_values(rng, shape, spread, most, pieces=(), kind=jnp.bfloat16):
    drawn = jax.random.normal(rng, shape, jnp.float32) * spread
    if len(pieces) > 0:
        drawn = levels(rng, shape, pieces, -0.22, 0.18) * drawn
    return jnp.clip(drawn, min=-most, max=most).astype(kind)


def bell_draw_with(stream_key, extent, width, bound, pieces, heavy, kind=jnp.bfloat16):
    drawn = width * jax.random.normal(stream_key, extent, jnp.float32)
    if pieces:
        drawn = drawn * levels(stream_key, extent, pieces, -0.22, 0.18)
    return jnp.clip(strengthened(drawn, jax.random.fold_in(stream_key, 3), *heavy), -bound, bound).astype(kind)


def setup_inputs(seed: int = 0) -> dict:
    key_list = jax.random.split(jax.random.key(seed), 7)
    return {
        "tokens": normal_values(key_list[0], (LENGTH, D), 1.0, 6.0, ((0, 8), (1, 64))),
        "in_values": bell_draw_with(key_list[1], (D, 3, D), D ** -0.5, 0.1875, ((0, 8), (2, 64)), (2, 0, 64, 4.0)),
        "in_scales": jnp.clip(jnp.exp(math.log(2.0) - 1.3862944 * jax.random.uniform(key_list[2], (D // BLOCK, 3, D), jnp.float32) ** levels(key_list[2], (D // BLOCK, 3, D), ((0, 8), (2, 64)), -0.2, 0.2)), 0.5, 2.0).astype(jnp.bfloat16),
        "filters": draw_filters(jax.random.fold_in(key_list[6], 71), 0),
        "out_weight": normal_values(key_list[4], (D, D), D ** -0.5, 0.0625, ((0, 64), (1, 8))),
        "cotangent": draw_cotangent(jax.random.fold_in(key_list[6], 71), 0),
    }


def dequantize(values, scales):
    scaled = values.astype(jnp.float32).reshape(D // BLOCK, BLOCK, 3, D) * scales.astype(jnp.float32)[:, None]
    return scaled.reshape(D, 3 * D).astype(jnp.bfloat16)


def reference(tokens, in_values, in_scales, filters, out_weight, cotangent):
    length = tokens.shape[0]
    weight = dequantize(in_values, in_scales)
    proj = jnp.dot(tokens, weight, preferred_element_type=jnp.float32).astype(jnp.bfloat16).reshape(length, 3, D)
    query = proj[:, 0].astype(jnp.float32)
    key_part = proj[:, 1].astype(jnp.float32)
    value_part = proj[:, 2].astype(jnp.float32)
    product = key_part * value_part
    repeated = jnp.repeat(filters, GROUP, axis=0)
    padded_past = jnp.concatenate([jnp.zeros((TAPS - 1, D), jnp.float32), product], 0)

    def causal_step(lag_index, total):
        offset = (TAPS - 1 - lag_index).astype(jnp.int32)
        slab = lax.dynamic_slice_in_dim(padded_past, offset, length, 0)
        column = lax.dynamic_slice_in_dim(repeated, jnp.asarray(lag_index).astype(jnp.int32), 1, 1)[:, 0]
        return total + column[None, :] * slab

    conv = lax.fori_loop(0, TAPS, causal_step, jnp.zeros((length, D), jnp.float32))
    grad_z = jnp.dot(cotangent, out_weight.T, preferred_element_type=jnp.float32)
    grad_query = grad_z * conv
    grad_conv = grad_z * query
    padded_next = jnp.concatenate([grad_conv, jnp.zeros((TAPS - 1, D), jnp.float32)], 0)

    def later_step(lag_index, total):
        offset = jnp.asarray(lag_index).astype(jnp.int32)
        slab = lax.dynamic_slice_in_dim(padded_next, offset, length, 0)
        column = lax.dynamic_slice_in_dim(repeated, offset, 1, 1)[:, 0]
        return total + column[None, :] * slab

    grad_product = lax.fori_loop(0, TAPS, later_step, jnp.zeros((length, D), jnp.float32))
    grad_proj = jnp.stack([grad_query, grad_product * value_part, grad_product * key_part], axis=1)
    grad_proj = grad_proj.astype(jnp.bfloat16).reshape(length, 3 * D)
    input_grad = jnp.dot(grad_proj, weight.T, preferred_element_type=jnp.float32).astype(jnp.bfloat16)

    def one_lag(lag_index):
        offset = (TAPS - 1 - lag_index).astype(jnp.int32)
        slab = lax.dynamic_slice_in_dim(padded_past, offset, length, 0)
        return jnp.sum((grad_conv * slab).reshape(length, D // GROUP, GROUP), axis=(0, 2))

    per_lag = lax.map(one_lag, jnp.arange(TAPS, dtype=jnp.int32))
    filter_grad = per_lag.T / TOK_DEV
    return input_grad, filter_grad
```

```python
import functools

import jax
import jax.numpy as jnp
from jax import lax
from jax.experimental import pallas as pl
from jax.experimental.pallas import tpu as pltpu
from jax.sharding import PartitionSpec as P

MESH = pl.DeviceIdType.MESH
BLOCK = 128
GROUP = 16
PIECES = 8
UP, DOWN = 0, 1


def piece_at(position):
    odd_node, core, half = position // 4, (position // 2) % 2, position % 2
    return 4 * odd_node + 2 * half + 1 - core


def dot(a, b, contract, precision=None):
    return lax.dot_general(
        a, b, ((contract[:1], contract[1:]), ((), ())),
        preferred_element_type=jnp.float32, precision=precision,
    )


def exact(a, b, contract):
    return dot(a, b, contract, lax.Precision.HIGHEST)


def kernel(
    n_f, n_z,
    tok, cot, val, scl, flt, out_w,
    input_grad, filter_grad,
    tok_all, cot_all, wt, wn, ow, part, gz_part, part_in, gz_in, gp, fg_all,
    own, pair_out, pair_in, ring_out, ring_in, last_out, last_in,
    perm_s, perm_r, ring_s, ring_r, core_s, core_r, rs_s, rs_r, ag_s, ag_r, fg_s, fg_r,
    pair_s, pair_r, sum_s, sum_r, last_s, last_r,
):
    channels = val.shape[2]
    f, m = lax.axis_index("fsdp"), lax.axis_index("tensor")
    c, z, xh = lax.rem(m, 2), lax.rem(m // 2, n_z), m // (2 * n_z)
    along = lambda by: lax.rem(z + by + 2 * n_z, n_z)
    up = (xh * n_z + along(1)) * 2 + c
    down = (xh * n_z + along(-1)) * 2 + c
    other = m + 1 - 2 * c
    peer = lambda k: lax.rem(f + k, n_f)

    jm = lax.rem(m, PIECES)
    to_f, to_z, to_c, to_half = m // PIECES, 2 * f + jm // 4, 1 - lax.rem(jm, 2), lax.rem(jm, 4) // 2
    to_m = lambda x: (x * n_z + to_z) * 2 + to_c
    from_f = z // 2
    from_m = lambda half: PIECES * f + 4 * lax.rem(z, 2) + 2 * half + 1 - c

    def remote(src, dst, send, recv, fsdp, tensor):
        return pltpu.make_async_remote_copy(
            src_ref=src, dst_ref=dst, send_sem=send, recv_sem=recv,
            device_id={"fsdp": fsdp, "tensor": tensor}, device_id_type=MESH,
        )

    sent = []

    def start(copy):
        copy.start()
        sent.append(copy)

    barrier = pltpu.get_barrier_semaphore()
    greeted = [(f, up), (f, down), (f, other)]
    greeted += [(peer(k), m) for k in range(1, n_f)]
    greeted += [(to_f, to_m(x)) for x in range(2)]
    greeted += [(from_f, from_m(h)) for h in range(2)]
    for fsdp, tensor in greeted:
        pl.semaphore_signal(
            barrier, inc=1, device_id={"fsdp": fsdp, "tensor": tensor}, device_id_type=MESH
        )
    pl.semaphore_wait(barrier, len(greeted))

    gathered = (tok_all, cot_all)
    for a, block in enumerate((tok, cot)):
        for x in range(2):
            start(remote(
                block, gathered[a].at[to_z, to_c, to_half],
                perm_s.at[a, x], perm_r.at[a, to_half], to_f, to_m(x),
            ))

    for position in range(PIECES):
        piece = piece_at(position)
        rows = slice(position * BLOCK, (position + 1) * BLOCK)
        for j in range(3):
            scaled = val[j, piece * BLOCK : (piece + 1) * BLOCK, :].astype(jnp.float32) * scl[
                j, piece : piece + 1, :
            ].astype(jnp.float32)
            columns = slice(j * channels, (j + 1) * channels)
            wn[rows, columns] = scaled.astype(jnp.bfloat16)
            wt[columns, rows] = scaled.T.astype(jnp.bfloat16)
        ow[:, rows] = out_w[:, piece * BLOCK : (piece + 1) * BLOCK]

    steps = ((n_z // 2, n_z // 2 - 1), (n_z // 2 - 1, n_z // 2))

    def ring(a, way, step):
        slot = along(-step if way == UP else step)
        chunk = gathered[a].at[slot, c]
        return remote(
            chunk, chunk, ring_s.at[a, way, step], ring_r.at[a, way, step],
            f, up if way == UP else down,
        )

    def landed(a, way, step):
        slot = along(-step - 1 if way == UP else step + 1)
        chunk = gathered[a].at[slot, c]
        return remote(
            chunk, chunk, ring_s.at[a, way, step], ring_r.at[a, way, step],
            f, up if way == UP else down,
        )

    def order(a):
        return [(0, 0)] + [(1 + s, -s - 1) for s in range(steps[a][UP])] + [
            (1 + steps[a][UP] + s, s + 1) for s in range(steps[a][DOWN])
        ]

    def across(a, index, by, core):
        chunk = gathered[a].at[along(by), core]
        return remote(chunk, chunk, core_s.at[a, index], core_r.at[a, index], f, other)

    for a in range(2):
        for half in range(2):
            block = gathered[a].at[z, c, half]
            remote(block, block, perm_s.at[a, half], perm_r.at[a, half], f, other).wait_recv()
        for way in (UP, DOWN):
            start(ring(a, way, 0))
        start(across(a, 0, 0, c))
    for step in range(n_z // 2):
        for a in range(2):
            for way in (UP, DOWN):
                if step < steps[a][way]:
                    landed(a, way, step).wait_recv()
                    if step + 1 < steps[a][way]:
                        start(ring(a, way, step + 1))
                    if way == UP:
                        start(across(a, 1 + step, -step - 1, c))
                    else:
                        start(across(a, 1 + steps[a][UP] + step, step + 1, c))
    for a in range(2):
        for index, by in order(a):
            across(a, index, by, 1 - c).wait_recv()

    def gathered_rows(buffer, tb):
        blocks = [buffer[2 * tb + n, core, half] for n in range(2) for core in range(2) for half in range(2)]
        return jnp.concatenate(blocks, axis=1)

    def forward(tb, carry):
        columns = pl.ds(pl.multiple_of(tb * BLOCK, BLOCK), BLOCK)
        proj = dot(wt[...], gathered_rows(tok_all, tb), (1, 1)).astype(jnp.bfloat16)
        for j in range(3):
            part[j, :, columns] = proj[j * channels : (j + 1) * channels]
        gz_part[:, columns] = dot(ow[...], gathered_rows(cot_all, tb), (1, 1)).astype(jnp.bfloat16)
        return carry

    lax.fori_loop(0, n_f, forward, 0)

    group_rows = lambda g: pl.ds(pl.multiple_of(g * GROUP, GROUP), GROUP)

    def scatter(k):
        return (
            remote(part.at[:, group_rows(peer(k)), :], part_in.at[k - 1], rs_s.at[0, k - 1], rs_r.at[0, k - 1], peer(k), m),
            remote(gz_part.at[group_rows(peer(k)), :], gz_in.at[k - 1], rs_s.at[1, k - 1], rs_r.at[1, k - 1], peer(k), m),
        )

    for k in range(1, n_f):
        for copy in scatter(k):
            start(copy)
    mine = group_rows(f)
    proj_sum = part[:, mine, :].astype(jnp.float32)
    gz_sum = gz_part[mine, :].astype(jnp.float32)
    for k in range(1, n_f):
        for copy in scatter(k):
            copy.wait_recv()
        proj_sum = proj_sum + part_in[k - 1].astype(jnp.float32)
        gz_sum = gz_sum + gz_in[k - 1].astype(jnp.float32)

    def stacked(x):
        return jnp.concatenate([x[:, b * BLOCK : (b + 1) * BLOCK] for b in range(n_f)], axis=0)

    def unstacked(x):
        return jnp.concatenate([x[b * GROUP : (b + 1) * GROUP] for b in range(n_f)], axis=1)

    proj_sum = proj_sum.astype(jnp.bfloat16).astype(jnp.float32)
    query, key, value = (stacked(proj_sum[j]) for j in range(3))
    grad_z = stacked(gz_sum)
    nothing = jnp.zeros((GROUP, BLOCK), jnp.float32)
    product = key * value
    before = jnp.concatenate([nothing, product[:-GROUP]], axis=0)
    taps = jnp.concatenate([flt[pl.ds(f, 1), :], jnp.zeros((1, BLOCK), jnp.float32)], axis=1)
    band = pltpu.roll(jnp.broadcast_to(taps, (BLOCK, 2 * BLOCK)), 0, 1, stride=1, stride_axis=0)
    band_here, band_next = band[:, :BLOCK], band[:, BLOCK:]
    conv = exact(product, band_here, (1, 0)) + exact(before, band_next, (1, 0))
    grad_query = grad_z * conv
    grad_conv = grad_z * query
    after = jnp.concatenate([grad_conv[GROUP:], nothing], axis=0)
    grad_product = exact(grad_conv, band_here, (1, 1)) + exact(after, band_next, (1, 1))
    for j, grad in enumerate((grad_query, grad_product * value, grad_product * key)):
        gp[j, mine, :] = unstacked(grad).astype(jnp.bfloat16)

    def share(k, owner):
        rows = gp.at[:, group_rows(owner), :]
        return remote(rows, rows, ag_s.at[k - 1], ag_r.at[k - 1], peer(k), m)

    for k in range(1, n_f):
        start(share(k, f))

    flip = (
        lax.broadcasted_iota(jnp.int32, (BLOCK, BLOCK), 0)
        + lax.broadcasted_iota(jnp.int32, (BLOCK, BLOCK), 1)
        == BLOCK - 1
    ).astype(jnp.float32)
    turned = exact(product, flip, (1, 0))
    corr = exact(turned, jnp.concatenate([grad_conv, after], axis=1), (0, 0))
    skewed = pltpu.roll(corr, 0, 1, stride=1, stride_axis=0)
    lags = pltpu.roll(jnp.sum(skewed, axis=0, keepdims=True), BLOCK + 1, 1)[:, :BLOCK]
    fg_all[f] = jnp.broadcast_to(lags * (1.0 / BLOCK), (8, BLOCK))

    def share_filter(k, owner):
        return remote(fg_all.at[owner], fg_all.at[owner], fg_s.at[k - 1], fg_r.at[k - 1], peer(k), m)

    for k in range(1, n_f):
        start(share_filter(k, f))
    for k in range(1, n_f):
        share(k, peer(n_f - k)).wait_recv()

    wide = 2 * BLOCK

    def backward(i, core):
        columns = pl.ds(pl.multiple_of(i * wide, wide), wide)
        grads = jnp.concatenate([gp[j, :, columns] for j in range(3)], axis=0)
        return [
            dot(wn[pl.ds(pl.multiple_of((4 * n + 2 * core) * BLOCK, wide), wide), :], grads, (1, 0))
            for n in range(2)
        ]

    def pair(i):
        chunks = pl.ds(4 * i, 4)
        return remote(pair_out.at[chunks], pair_in.at[chunks], pair_s.at[i], pair_r.at[i], f, other)

    for i in range(n_f // 2):
        halves = backward(i, 1 - c)
        for t in range(2):
            for n in range(2):
                pair_out[4 * i + 2 * t + n] = halves[n][:, t * BLOCK : (t + 1) * BLOCK].astype(jnp.bfloat16)
        start(pair(i))
    for i in range(n_f // 2):
        halves = backward(i, c)
        for t in range(2):
            for n in range(2):
                own[4 * i + 2 * t + n] = halves[n][:, t * BLOCK : (t + 1) * BLOCK]
    for i in range(n_f // 2):
        pair(i).wait_recv()

    hops = (n_z // 2, n_z // 2 - 1)

    def pass_on(way, step):
        return remote(
            ring_out.at[way, step], ring_in.at[way, step], sum_s.at[way, step], sum_r.at[way, step],
            f, up if way == UP else down,
        )

    for step in range(n_z // 2):
        for way in (UP, DOWN):
            if step < hops[way]:
                slot = along(hops[UP] - step if way == UP else step - hops[DOWN])
                total = own[slot] + pair_in[slot].astype(jnp.float32)
                if step > 0:
                    pass_on(way, step - 1).wait_recv()
                    total = total + ring_in[way, step - 1].astype(jnp.float32)
                ring_out[way, step] = total.astype(jnp.bfloat16)
                start(pass_on(way, step))
    total = own[z] + pair_in[z].astype(jnp.float32)
    for way in (UP, DOWN):
        pass_on(way, hops[way] - 1).wait_recv()
        total = total + ring_in[way, hops[way] - 1].astype(jnp.float32)

    for half in range(2):
        last_out[half] = total[half * BLOCK : (half + 1) * BLOCK].astype(jnp.bfloat16)
        start(remote(
            last_out.at[half], last_in.at[xh], last_s.at[half], last_r.at[xh], from_f, from_m(half)
        ))
    for x in range(2):
        remote(last_out.at[x], last_in.at[x], last_s.at[x], last_r.at[x], to_f, to_m(x)).wait_recv()
    summed = last_in[0].astype(jnp.float32) + last_in[1].astype(jnp.float32)
    input_grad[...] = summed.T.astype(jnp.bfloat16)

    for k in range(1, n_f):
        share_filter(k, peer(n_f - k)).wait_recv()
    filter_grad[...] = jnp.concatenate([fg_all[g, 0:1, :] for g in range(n_f)], axis=0)
    for copy in sent:
        copy.wait_send()


def on_device(n_f, n_z, tokens, in_values, in_scales, filters, out_weight, cotangent):
    channels = in_values.shape[2]
    features = PIECES * BLOCK
    length = n_f * BLOCK
    bf16, f32 = jnp.bfloat16, jnp.float32
    dma = pltpu.SemaphoreType.DMA
    return pl.pallas_call(
        functools.partial(kernel, n_f, n_z),
        out_shape=(
            jax.ShapeDtypeStruct((BLOCK, BLOCK), bf16),
            jax.ShapeDtypeStruct((n_f, BLOCK), f32),
        ),
        in_specs=[pl.BlockSpec(memory_space=pltpu.VMEM)] * 6,
        out_specs=(pl.BlockSpec(memory_space=pltpu.VMEM),) * 2,
        scratch_shapes=[
            pltpu.VMEM((n_z, 2, 2, BLOCK, BLOCK), bf16),
            pltpu.VMEM((n_z, 2, 2, BLOCK, BLOCK), bf16),
            pltpu.VMEM((3 * channels, features), bf16),
            pltpu.VMEM((features, 3 * channels), bf16),
            pltpu.VMEM((channels, features), bf16),
            pltpu.VMEM((3, channels, length), bf16),
            pltpu.VMEM((channels, length), bf16),
            pltpu.VMEM((n_f - 1, 3, GROUP, length), bf16),
            pltpu.VMEM((n_f - 1, GROUP, length), bf16),
            pltpu.VMEM((3, channels, length), bf16),
            pltpu.VMEM((n_f, 8, BLOCK), f32),
            pltpu.VMEM((n_z, 2 * BLOCK, BLOCK), f32),
            pltpu.VMEM((n_z, 2 * BLOCK, BLOCK), bf16),
            pltpu.VMEM((n_z, 2 * BLOCK, BLOCK), bf16),
            pltpu.VMEM((2, n_z // 2, 2 * BLOCK, BLOCK), bf16),
            pltpu.VMEM((2, n_z // 2, 2 * BLOCK, BLOCK), bf16),
            pltpu.VMEM((2, BLOCK, BLOCK), bf16),
            pltpu.VMEM((2, BLOCK, BLOCK), bf16),
            dma((2, 2)), dma((2, 2)),
            dma((2, 2, n_z // 2)), dma((2, 2, n_z // 2)),
            dma((2, n_z)), dma((2, n_z)),
            dma((2, n_f - 1)), dma((2, n_f - 1)),
            dma((n_f - 1,)), dma((n_f - 1,)),
            dma((n_f - 1,)), dma((n_f - 1,)),
            dma((n_f // 2,)), dma((n_f // 2,)),
            dma((2, n_z // 2)), dma((2, n_z // 2)),
            dma((2,)), dma((2,)),
        ],
        compiler_params=pltpu.CompilerParams(
            collective_id=0, has_side_effects=True, vmem_limit_bytes=48 << 20
        ),
        name="hyena",
    )(
        tokens, cotangent, in_values.transpose(1, 0, 2), in_scales.transpose(1, 0, 2),
        filters, out_weight,
    )


def solution(mesh):
    placed = (
        P("fsdp", "tensor"),
        P("fsdp", None, "tensor"),
        P("fsdp", None, "tensor"),
        P("tensor", None),
        P("tensor", "fsdp"),
        P("fsdp", "tensor"),
    )
    return jax.shard_map(
        functools.partial(on_device, mesh.shape["fsdp"], mesh.shape["tensor"] // 4),
        mesh=mesh,
        in_specs=placed,
        out_specs=(P("fsdp", "tensor"), P("tensor", None)),
        check_vma=False,
    )
```

```python
import functools

import jax
import jax.numpy as jnp
from jax import lax
from jax.experimental import pallas as pl
from jax.experimental.pallas import tpu as pltpu
from jax.sharding import PartitionSpec as P

MESH = pl.DeviceIdType.MESH
BLOCK = 128
GROUP = 16
PIECES = 8
UP, DOWN = 0, 1


def piece_at(position):
    odd_node, core, half = position // 4, (position // 2) % 2, position % 2
    return 4 * odd_node + 2 * half + 1 - core


def dot(a, b, contract, precision=None):
    return lax.dot_general(
        a, b, ((contract[:1], contract[1:]), ((), ())),
        preferred_element_type=jnp.float32, precision=precision,
    )


def exact(a, b, contract):
    return dot(a, b, contract, lax.Precision.HIGHEST)


def kernel(
    n_f, n_z,
    tok, cot, val_hbm, scl_hbm, flt_hbm, out_w_hbm,
    input_grad, filter_grad,
    val, scl, flt, out_w, gathered, wt, wn, ow, part, part_in, gp, fg_all,
    own, pair_out, pair_in, ring_out, ring_in, last_out, last_in,
    in_s, perm_s, perm_r, ring_s, ring_r, slice_s, slice_r, core_s, core_r, rs_s, rs_r, ag_s, ag_r, fg_s, fg_r,
    pair_s, pair_r, sum_s, sum_r, last_s, last_r,
):
    channels = val.shape[2]
    half_z, half_f = n_z // 2, n_f // 2
    f, m = lax.axis_index("fsdp"), lax.axis_index("tensor")
    c, z, xh = lax.rem(m, 2), lax.rem(m // 2, n_z), m // (2 * n_z)
    along = lambda by: lax.rem(z + by + 2 * n_z, n_z)
    up = (xh * n_z + along(1)) * 2 + c
    down = (xh * n_z + along(-1)) * 2 + c
    other = m + 1 - 2 * c
    across_x = ((1 - xh) * n_z + z) * 2 + c
    peer = lambda k: lax.rem(f + k, n_f)
    tokens_at = lambda off: lax.rem(z // 2 + off + n_f, n_f)

    jm = lax.rem(m, PIECES)
    to_f, to_z, to_c, to_half = m // PIECES, 2 * f + jm // 4, 1 - lax.rem(jm, 2), lax.rem(jm, 4) // 2
    to_m = lambda x: (x * n_z + to_z) * 2 + to_c
    from_f = z // 2
    from_m = lambda half: PIECES * f + 4 * lax.rem(z, 2) + 2 * half + 1 - c

    def remote(src, dst, send, recv, fsdp, tensor):
        return pltpu.make_async_remote_copy(
            src_ref=src, dst_ref=dst, send_sem=send, recv_sem=recv,
            device_id={"fsdp": fsdp, "tensor": tensor}, device_id_type=MESH,
        )

    sent = []

    def start(copy):
        copy.start()
        sent.append(copy)

    loads = [
        pltpu.make_async_copy(src, dst, in_s.at[i])
        for i, (src, dst) in enumerate(
            ((val_hbm, val), (scl_hbm, scl), (flt_hbm, flt), (out_w_hbm, out_w))
        )
    ]
    for load in loads:
        load.start()
    barrier = pltpu.get_barrier_semaphore()
    greeted = [(f, up), (f, down), (f, other), (f, across_x)]
    greeted += [(peer(k), m) for k in range(1, n_f)]
    greeted += [(to_f, to_m(x)) for x in range(2)]
    greeted += [(from_f, from_m(h)) for h in range(2)]
    for fsdp, tensor in greeted:
        pl.semaphore_signal(
            barrier, inc=1, device_id={"fsdp": fsdp, "tensor": tensor}, device_id_type=MESH
        )
    pl.semaphore_wait(barrier, len(greeted))

    for a, block in enumerate((tok, cot)):
        start(remote(
            block, gathered.at[to_z, to_c, to_half, a], perm_s.at[a], perm_r.at[a], to_f, to_m(to_half)
        ))

    for load in loads:
        load.wait()
    for position in range(PIECES):
        piece = piece_at(position)
        rows = slice(position * BLOCK, (position + 1) * BLOCK)
        for j in range(3):
            scaled = val[j, piece * BLOCK : (piece + 1) * BLOCK, :].astype(jnp.float32) * scl[
                j, piece : piece + 1, :
            ].astype(jnp.float32)
            columns = slice(j * channels, (j + 1) * channels)
            wn[rows, columns] = scaled.astype(jnp.bfloat16)
            wt[columns, rows] = scaled.T.astype(jnp.bfloat16)
        ow[:, rows] = out_w[:, piece * BLOCK : (piece + 1) * BLOCK]

    steps = ((half_z, half_z - 1), (half_z - 1, half_z))

    def ring(a, way, step, ahead=0):
        slot = along(-step - ahead if way == UP else step + ahead)
        chunk = gathered.at[slot, c, xh, a]
        return remote(
            chunk, chunk, ring_s.at[a, way, step], ring_r.at[a, way, step],
            f, up if way == UP else down,
        )

    def over_x(by, half):
        chunk = gathered.at[along(by), c, half]
        return remote(chunk, chunk, slice_s.at[by % n_z], slice_r.at[by % n_z], f, across_x)

    def over_core(by, half, which, core):
        chunk = gathered.at[along(by), core, half]
        return remote(chunk, chunk, core_s.at[which, by % n_z], core_r.at[which, by % n_z], f, other)

    def nodes_at(distance):
        return [distance] if distance in (0, half_z) else [-distance, distance]

    def rows_of(tb, a):
        blocks = [gathered[2 * tb + n, core, half, a] for n in range(2) for core in range(2) for half in range(2)]
        return jnp.concatenate(blocks, axis=1)

    group_rows = lambda g: pl.ds(pl.multiple_of(g * GROUP, GROUP), GROUP)

    def scatter(k, off):
        return remote(
            part.at[tokens_at(off), :, group_rows(peer(k)), :], part_in.at[k - 1, tokens_at(off)],
            rs_s.at[k - 1, off % n_f], rs_r.at[k - 1, off % n_f], peer(k), m,
        )

    def products(distance):
        for d in (2 * distance, 2 * distance + 1):
            if d <= half_z:
                for by in nodes_at(d):
                    over_core(by, xh, 0, 1 - c).wait_recv()
                    over_core(by, 1 - xh, 1, 1 - c).wait_recv()
        for off in [distance] if distance in (0, half_f) else [-distance, distance]:
            tb = tokens_at(off)
            proj = dot(wt[...], rows_of(tb, 0), (1, 1)).astype(jnp.bfloat16)
            for j in range(3):
                part[tb, j] = proj[j * channels : (j + 1) * channels]
            part[tb, 3] = dot(ow[...], rows_of(tb, 1), (1, 1)).astype(jnp.bfloat16)
            for k in range(1, n_f):
                start(scatter(k, off))

    for a in range(2):
        block = gathered.at[z, c, xh, a]
        remote(block, block, perm_s.at[a], perm_r.at[a], f, other).wait_recv()
        for way in (UP, DOWN):
            start(ring(a, way, 0))
    start(over_x(0, xh))
    start(over_core(0, xh, 0, c))
    done = 0
    for step in range(half_z):
        for a in range(2):
            for way in (UP, DOWN):
                if step < steps[a][way]:
                    ring(a, way, step, 1).wait_recv()
                    if step + 1 < steps[a][way]:
                        start(ring(a, way, step + 1))
        for by in nodes_at(step + 1):
            start(over_x(by, xh))
            start(over_core(by, xh, 0, c))
        for by in nodes_at(step):
            over_x(by, 1 - xh).wait_recv()
            start(over_core(by, 1 - xh, 1, c))
        if step == 2 * done + 2:
            products(done)
            done += 1
    for by in nodes_at(half_z):
        over_x(by, 1 - xh).wait_recv()
        start(over_core(by, 1 - xh, 1, c))
    for distance in range(done, half_f + 1):
        products(distance)

    mine = group_rows(f)
    offsets = [off for d in range(half_f + 1) for off in ([d] if d in (0, half_f) else [-d, d])]
    taps = jnp.concatenate([flt[pl.ds(f, 1), :], jnp.zeros((1, BLOCK), jnp.float32)], axis=1)
    band = pltpu.roll(jnp.broadcast_to(taps, (BLOCK, 2 * BLOCK)), 0, 1, stride=1, stride_axis=0)
    band_here, band_next = band[:, :BLOCK], band[:, BLOCK:]
    for off in offsets:
        for k in range(1, n_f):
            scatter(k, off).wait_recv()

    def summed_part(j):
        total = part[:, j, mine, :].astype(jnp.float32)
        for k in range(1, n_f):
            total = total + part_in[k - 1, :, j].astype(jnp.float32)
        return total.reshape(n_f * GROUP, BLOCK)

    query, key, value = (
        summed_part(j).astype(jnp.bfloat16).astype(jnp.float32) for j in range(3)
    )
    grad_z = summed_part(3)
    nothing = jnp.zeros((GROUP, BLOCK), jnp.float32)
    product = key * value
    before = jnp.concatenate([nothing, product[:-GROUP]], axis=0)
    conv = exact(product, band_here, (1, 0)) + exact(before, band_next, (1, 0))
    grad_query = grad_z * conv
    grad_conv = grad_z * query
    after = jnp.concatenate([grad_conv[GROUP:], nothing], axis=0)
    grad_product = exact(grad_conv, band_here, (1, 1)) + exact(after, band_next, (1, 1))
    for j, grad in enumerate((grad_query, grad_product * value, grad_product * key)):
        gp[:, j, mine, :] = grad.astype(jnp.bfloat16).reshape(n_f, GROUP, BLOCK)

    hops = (half_z, half_z - 1)
    needed = []
    for step in range(half_z):
        fresh = []
        for odd in range(2):
            for node in [odd + half_z - step] + ([odd - hops[DOWN] + step] if step < hops[DOWN] else []):
                off = (node // 2) % n_f
                if off not in fresh and all(off not in seen for seen in needed):
                    fresh.append(off)
        needed.append(fresh)
    if all(0 not in seen for seen in needed):
        needed[-1].append(0)

    def share(k, off, owner):
        rows = gp.at[tokens_at(off), :, group_rows(owner), :]
        return remote(rows, rows, ag_s.at[k - 1, off], ag_r.at[k - 1, off], peer(k), m)

    for fresh in needed:
        for off in fresh:
            for k in range(1, n_f):
                start(share(k, off, f))

    flip = (
        lax.broadcasted_iota(jnp.int32, (BLOCK, BLOCK), 0)
        + lax.broadcasted_iota(jnp.int32, (BLOCK, BLOCK), 1)
        == BLOCK - 1
    ).astype(jnp.float32)
    turned = exact(product, flip, (1, 0))
    corr = exact(turned, jnp.concatenate([grad_conv, after], axis=1), (0, 0))
    skewed = pltpu.roll(corr, 0, 1, stride=1, stride_axis=0)
    lags = pltpu.roll(jnp.sum(skewed, axis=0, keepdims=True), BLOCK + 1, 1)[:, :BLOCK]
    fg_all[f] = jnp.broadcast_to(lags * (1.0 / BLOCK), (8, BLOCK))

    def share_filter(k, owner):
        return remote(fg_all.at[owner], fg_all.at[owner], fg_s.at[k - 1], fg_r.at[k - 1], peer(k), m)

    def pair(off):
        chunks = pl.ds(2 * tokens_at(off), 2)
        return remote(pair_out.at[chunks], pair_in.at[chunks], pair_s.at[off], pair_r.at[off], f, other)

    def backward(off):
        for k in range(1, n_f):
            share(k, off, peer(n_f - k)).wait_recv()
        tb = tokens_at(off)
        grads = jnp.concatenate([gp[tb, j] for j in range(3)], axis=0)

        def rows_for(n, core):
            rows = pl.ds(pl.multiple_of((4 * n + 2 * core) * BLOCK, 2 * BLOCK), 2 * BLOCK)
            return dot(wn[rows, :], grads, (1, 0))

        for n in range(2):
            pair_out[2 * tb + n] = rows_for(n, 1 - c).astype(jnp.bfloat16)
        start(pair(off))
        for n in range(2):
            own[2 * tb + n] = rows_for(n, c)

    def pass_on(way, step, half):
        return remote(
            ring_out.at[way, step, half], ring_in.at[way, step, half],
            sum_s.at[way, step, half], sum_r.at[way, step, half], f, up if way == UP else down,
        )

    def local(slot, half):
        rows = slice(half * BLOCK, (half + 1) * BLOCK)
        return own[slot, rows, :] + pair_in[slot, rows, :].astype(jnp.float32)

    for off in needed[0]:
        backward(off)
    for step in range(half_z):
        for off in needed[step]:
            pair(off).wait_recv()
        for way in (UP, DOWN):
            if step < hops[way]:
                slot = along(half_z - step if way == UP else step - hops[DOWN])
                for half in range(2):
                    total = local(slot, half)
                    if step > 0:
                        pass_on(way, step - 1, half).wait_recv()
                        total = total + ring_in[way, step - 1, half].astype(jnp.float32)
                    ring_out[way, step, half] = total.astype(jnp.bfloat16)
                    start(pass_on(way, step, half))
        if step == 0:
            for k in range(1, n_f):
                start(share_filter(k, f))
        if step + 1 < half_z:
            for off in needed[step + 1]:
                backward(off)

    for half in range(2):
        total = local(z, half)
        for way in (UP, DOWN):
            pass_on(way, hops[way] - 1, half).wait_recv()
            total = total + ring_in[way, hops[way] - 1, half].astype(jnp.float32)
        last_out[half] = total.astype(jnp.bfloat16)
        start(remote(
            last_out.at[half], last_in.at[xh], last_s.at[half], last_r.at[xh], from_f, from_m(half)
        ))
    for k in range(1, n_f):
        share_filter(k, peer(n_f - k)).wait_recv()
    filter_grad[...] = jnp.concatenate([fg_all[g, 0:1, :] for g in range(n_f)], axis=0)
    for x in range(2):
        remote(last_out.at[x], last_in.at[x], last_s.at[x], last_r.at[x], to_f, to_m(x)).wait_recv()
    summed = last_in[0].astype(jnp.float32) + last_in[1].astype(jnp.float32)
    input_grad[...] = summed.T.astype(jnp.bfloat16)
    for copy in sent:
        copy.wait_send()


def on_device(n_f, n_z, tokens, in_values, in_scales, filters, out_weight, cotangent):
    channels = in_values.shape[2]
    features = PIECES * BLOCK
    bf16, f32 = jnp.bfloat16, jnp.float32
    dma = pltpu.SemaphoreType.DMA
    values, scales = in_values.transpose(1, 0, 2), in_scales.transpose(1, 0, 2)
    return pl.pallas_call(
        functools.partial(kernel, n_f, n_z),
        out_shape=(
            jax.ShapeDtypeStruct((BLOCK, BLOCK), bf16),
            jax.ShapeDtypeStruct((n_f, BLOCK), f32),
        ),
        in_specs=[pl.BlockSpec(memory_space=pl.ANY)] * 6,
        out_specs=(pl.BlockSpec(memory_space=pltpu.VMEM),) * 2,
        scratch_shapes=[
            pltpu.VMEM(values.shape, bf16),
            pltpu.VMEM(scales.shape, bf16),
            pltpu.VMEM(filters.shape, f32),
            pltpu.VMEM(out_weight.shape, bf16),
            pltpu.VMEM((n_z, 2, 2, 2, BLOCK, BLOCK), bf16),
            pltpu.VMEM((3 * channels, features), bf16),
            pltpu.VMEM((features, 3 * channels), bf16),
            pltpu.VMEM((channels, features), bf16),
            pltpu.VMEM((n_f, 4, channels, BLOCK), bf16),
            pltpu.VMEM((n_f - 1, n_f, 4, GROUP, BLOCK), bf16),
            pltpu.VMEM((n_f, 3, channels, BLOCK), bf16),
            pltpu.VMEM((n_f, 8, BLOCK), f32),
            pltpu.VMEM((n_z, 2 * BLOCK, BLOCK), f32),
            pltpu.VMEM((n_z, 2 * BLOCK, BLOCK), bf16),
            pltpu.VMEM((n_z, 2 * BLOCK, BLOCK), bf16),
            pltpu.VMEM((2, n_z // 2, 2, BLOCK, BLOCK), bf16),
            pltpu.VMEM((2, n_z // 2, 2, BLOCK, BLOCK), bf16),
            pltpu.VMEM((2, BLOCK, BLOCK), bf16),
            pltpu.VMEM((2, BLOCK, BLOCK), bf16),
            dma((4,)),
            dma((2,)), dma((2,)),
            dma((2, 2, n_z // 2)), dma((2, 2, n_z // 2)),
            dma((n_z,)), dma((n_z,)),
            dma((2, n_z)), dma((2, n_z)),
            dma((n_f - 1, n_f)), dma((n_f - 1, n_f)),
            dma((n_f - 1, n_f)), dma((n_f - 1, n_f)),
            dma((n_f - 1,)), dma((n_f - 1,)),
            dma((n_f,)), dma((n_f,)),
            dma((2, n_z // 2, 2)), dma((2, n_z // 2, 2)),
            dma((2,)), dma((2,)),
        ],
        compiler_params=pltpu.CompilerParams(
            collective_id=0, has_side_effects=True, vmem_limit_bytes=56 << 20
        ),
        name="hyena",
    )(tokens, cotangent, values, scales, filters, out_weight)


def solution(mesh):
    placed = (
        P("fsdp", "tensor"),
        P("fsdp", None, "tensor"),
        P("fsdp", None, "tensor"),
        P("tensor", None),
        P("tensor", "fsdp"),
        P("fsdp", "tensor"),
    )
    return jax.shard_map(
        functools.partial(on_device, mesh.shape["fsdp"], mesh.shape["tensor"] // 4),
        mesh=mesh,
        in_specs=placed,
        out_specs=(P("fsdp", "tensor"), P("tensor", None)),
        check_vma=False,
    )
```

```python
import functools

import jax
import jax.numpy as jnp
from jax import lax
from jax.experimental import pallas as pl
from jax.experimental.pallas import tpu as pltpu
from jax.sharding import PartitionSpec as P

MESH = pl.DeviceIdType.MESH
BLOCK = 128
GROUP = 16
PIECES = 8
UP, DOWN = 0, 1


def piece_at(position):
    odd_node, core, half = position // 4, (position // 2) % 2, position % 2
    return 4 * odd_node + 2 * half + 1 - core


def dot(a, b, contract, precision=None):
    return lax.dot_general(
        a, b, ((contract[:1], contract[1:]), ((), ())),
        preferred_element_type=jnp.float32, precision=precision,
    )


def exact(a, b, contract):
    return dot(a, b, contract, lax.Precision.HIGHEST)


def kernel(
    n_f, n_z,
    tok, cot, val_hbm, scl_hbm, flt_hbm, out_w_hbm,
    input_grad, filter_grad,
    val, scl, flt, out_w, gathered, wt, wn, ow, part, part_in, gp, fg_all,
    own, pair_out, pair_in, ring_out, ring_in, last_out, last_in,
    in_s, perm_s, perm_r, ring_s, ring_r, slice_s, slice_r, core_s, core_r, rs_s, rs_r, ag_s, ag_r, fg_s, fg_r,
    pair_s, pair_r, sum_s, sum_r, last_s, last_r,
):
    channels = val.shape[2]
    half_z, half_f = n_z // 2, n_f // 2
    f, m = lax.axis_index("fsdp"), lax.axis_index("tensor")
    c, z, xh = lax.rem(m, 2), lax.rem(m // 2, n_z), m // (2 * n_z)
    along = lambda by: lax.rem(z + by + 2 * n_z, n_z)
    up = (xh * n_z + along(1)) * 2 + c
    down = (xh * n_z + along(-1)) * 2 + c
    other = m + 1 - 2 * c
    across_x = ((1 - xh) * n_z + z) * 2 + c
    peer = lambda k: lax.rem(f + k, n_f)
    tokens_at = lambda off: lax.rem(z // 2 + off + n_f, n_f)

    jm = lax.rem(m, PIECES)
    to_f, to_z, to_c, to_half = m // PIECES, 2 * f + jm // 4, 1 - lax.rem(jm, 2), lax.rem(jm, 4) // 2
    to_m = lambda x: (x * n_z + to_z) * 2 + to_c
    from_f = z // 2
    from_m = lambda half: PIECES * f + 4 * lax.rem(z, 2) + 2 * half + 1 - c

    def remote(src, dst, send, recv, fsdp, tensor):
        return pltpu.make_async_remote_copy(
            src_ref=src, dst_ref=dst, send_sem=send, recv_sem=recv,
            device_id={"fsdp": fsdp, "tensor": tensor}, device_id_type=MESH,
        )

    sent = []

    def start(copy):
        copy.start()
        sent.append(copy)

    loads = [
        pltpu.make_async_copy(src, dst, in_s.at[i])
        for i, (src, dst) in enumerate(
            ((val_hbm, val), (scl_hbm, scl), (flt_hbm, flt), (out_w_hbm, out_w))
        )
    ]
    for load in loads:
        load.start()
    barrier = pltpu.get_barrier_semaphore()
    greeted = [(f, up), (f, down), (f, other), (f, across_x)]
    greeted += [(peer(k), m) for k in range(1, n_f)]
    greeted += [(to_f, to_m(x)) for x in range(2)]
    greeted += [(from_f, from_m(h)) for h in range(2)]
    for fsdp, tensor in greeted:
        pl.semaphore_signal(
            barrier, inc=1, device_id={"fsdp": fsdp, "tensor": tensor}, device_id_type=MESH
        )
    pl.semaphore_wait(barrier, len(greeted))

    for a, block in enumerate((tok, cot)):
        start(remote(
            block, gathered.at[to_z, to_c, to_half, a], perm_s.at[a], perm_r.at[a], to_f, to_m(to_half)
        ))

    for load in loads:
        load.wait()
    for position in range(PIECES):
        piece = piece_at(position)
        rows = slice(position * BLOCK, (position + 1) * BLOCK)
        for j in range(3):
            scaled = val[j, piece * BLOCK : (piece + 1) * BLOCK, :].astype(jnp.float32) * scl[
                j, piece : piece + 1, :
            ].astype(jnp.float32)
            columns = slice(j * channels, (j + 1) * channels)
            wn[rows, columns] = scaled.astype(jnp.bfloat16)
            wt[columns, rows] = scaled.T.astype(jnp.bfloat16)
        ow[:, rows] = out_w[:, piece * BLOCK : (piece + 1) * BLOCK]

    steps = ((half_z, half_z - 1), (half_z - 1, half_z), (half_z, half_z - 1))

    chains = ((0, xh), (1, xh), (0, 1 - xh))

    def ring(chain, way, step, ahead=0):
        slot = along(-step - ahead if way == UP else step + ahead)
        a, half = chains[chain]
        chunk = gathered.at[slot, c, half, a]
        return remote(
            chunk, chunk, ring_s.at[chain, way, step], ring_r.at[chain, way, step],
            f, up if way == UP else down,
        )

    def over_x(by, half):
        chunk = gathered.at[along(by), c, half, 1]
        return remote(chunk, chunk, slice_s.at[by % n_z], slice_r.at[by % n_z], f, across_x)

    def first_over_x(half):
        chunk = gathered.at[z, c, half, 0]
        return remote(chunk, chunk, slice_s.at[n_z], slice_r.at[n_z], f, across_x)

    def over_core(by, half, which, core):
        chunk = gathered.at[along(by), core, half]
        return remote(chunk, chunk, core_s.at[which, by % n_z], core_r.at[which, by % n_z], f, other)

    def nodes_at(distance):
        return [distance] if distance in (0, half_z) else [-distance, distance]

    def rows_of(tb, a):
        blocks = [gathered[2 * tb + n, core, half, a] for n in range(2) for core in range(2) for half in range(2)]
        return jnp.concatenate(blocks, axis=1)

    group_rows = lambda g: pl.ds(pl.multiple_of(g * GROUP, GROUP), GROUP)

    def scatter(k, off):
        return remote(
            part.at[tokens_at(off), :, group_rows(peer(k)), :], part_in.at[k - 1, tokens_at(off)],
            rs_s.at[k - 1, off % n_f], rs_r.at[k - 1, off % n_f], peer(k), m,
        )

    def products(distance):
        for d in (2 * distance, 2 * distance + 1):
            if d <= half_z:
                for by in nodes_at(d):
                    over_core(by, xh, 0, 1 - c).wait_recv()
                    over_core(by, 1 - xh, 1, 1 - c).wait_recv()
        for off in [distance] if distance in (0, half_f) else [-distance, distance]:
            tb = tokens_at(off)
            proj = dot(wt[...], rows_of(tb, 0), (1, 1)).astype(jnp.bfloat16)
            for j in range(3):
                part[tb, j] = proj[j * channels : (j + 1) * channels]
            part[tb, 3] = dot(ow[...], rows_of(tb, 1), (1, 1)).astype(jnp.bfloat16)
            for k in range(1, n_f):
                start(scatter(k, off))

    def arrived(chain, step):
        for way in (UP, DOWN):
            if step < steps[chain][way]:
                ring(chain, way, step, 1).wait_recv()
                if step + 1 < steps[chain][way]:
                    start(ring(chain, way, step + 1))

    for a in range(2):
        block = gathered.at[z, c, xh, a]
        remote(block, block, perm_s.at[a], perm_r.at[a], f, other).wait_recv()
        if a == 0:
            start(first_over_x(xh))
        for way in (UP, DOWN):
            start(ring(a, way, 0))
    start(over_x(0, xh))
    start(over_core(0, xh, 0, c))
    done = 0
    for step in range(half_z + 2):
        if step < half_z:
            for chain in range(2):
                arrived(chain, step)
            for by in nodes_at(step + 1):
                start(over_x(by, xh))
        if step == 0:
            first_over_x(1 - xh).wait_recv()
            for way in (UP, DOWN):
                start(ring(2, way, 0))
        if step >= 1:
            if step - 1 < half_z:
                arrived(2, step - 1)
            for by in nodes_at(step - 1):
                over_x(by, 1 - xh).wait_recv()
                start(over_core(by, 1 - xh, 1, c))
        if step < half_z:
            for by in nodes_at(step + 1):
                start(over_core(by, xh, 0, c))
        if step >= 2 * done + 3 and done < half_f:
            products(done)
            done += 1
    for distance in range(done, half_f + 1):
        products(distance)

    mine = group_rows(f)
    offsets = [off for d in range(half_f + 1) for off in ([d] if d in (0, half_f) else [-d, d])]
    taps = jnp.concatenate([flt[pl.ds(f, 1), :], jnp.zeros((1, BLOCK), jnp.float32)], axis=1)
    band = pltpu.roll(jnp.broadcast_to(taps, (BLOCK, 2 * BLOCK)), 0, 1, stride=1, stride_axis=0)
    band_here, band_next = band[:, :BLOCK], band[:, BLOCK:]
    for off in offsets:
        for k in range(1, n_f):
            scatter(k, off).wait_recv()

    def summed_part(j):
        total = part[:, j, mine, :].astype(jnp.float32)
        for k in range(1, n_f):
            total = total + part_in[k - 1, :, j].astype(jnp.float32)
        return total.reshape(n_f * GROUP, BLOCK)

    query, key, value = (
        summed_part(j).astype(jnp.bfloat16).astype(jnp.float32) for j in range(3)
    )
    grad_z = summed_part(3)
    nothing = jnp.zeros((GROUP, BLOCK), jnp.float32)
    product = key * value
    before = jnp.concatenate([nothing, product[:-GROUP]], axis=0)
    conv = exact(product, band_here, (1, 0)) + exact(before, band_next, (1, 0))
    grad_query = grad_z * conv
    grad_conv = grad_z * query
    after = jnp.concatenate([grad_conv[GROUP:], nothing], axis=0)
    grad_product = exact(grad_conv, band_here, (1, 1)) + exact(after, band_next, (1, 1))
    for j, grad in enumerate((grad_query, grad_product * value, grad_product * key)):
        gp[:, j, mine, :] = grad.astype(jnp.bfloat16).reshape(n_f, GROUP, BLOCK)

    hops = (half_z, half_z - 1)
    needed = []
    for step in range(half_z):
        fresh = []
        for odd in range(2):
            for node in [odd + half_z - step] + ([odd - hops[DOWN] + step] if step < hops[DOWN] else []):
                off = (node // 2) % n_f
                if off not in fresh and all(off not in seen for seen in needed):
                    fresh.append(off)
        needed.append(fresh)
    if all(0 not in seen for seen in needed):
        needed[-1].append(0)

    def share(k, off, owner):
        rows = gp.at[tokens_at(off), :, group_rows(owner), :]
        return remote(rows, rows, ag_s.at[k - 1, off], ag_r.at[k - 1, off], peer(k), m)

    for fresh in needed:
        for off in fresh:
            for k in range(1, n_f):
                start(share(k, off, f))

    flip = (
        lax.broadcasted_iota(jnp.int32, (BLOCK, BLOCK), 0)
        + lax.broadcasted_iota(jnp.int32, (BLOCK, BLOCK), 1)
        == BLOCK - 1
    ).astype(jnp.float32)
    turned = exact(product, flip, (1, 0))
    corr = exact(turned, jnp.concatenate([grad_conv, after], axis=1), (0, 0))
    skewed = pltpu.roll(corr, 0, 1, stride=1, stride_axis=0)
    lags = pltpu.roll(jnp.sum(skewed, axis=0, keepdims=True), BLOCK + 1, 1)[:, :BLOCK]
    fg_all[f] = jnp.broadcast_to(lags * (1.0 / BLOCK), (8, BLOCK))

    def share_filter(k, owner):
        return remote(fg_all.at[owner], fg_all.at[owner], fg_s.at[k - 1], fg_r.at[k - 1], peer(k), m)

    def pair(off):
        chunks = pl.ds(2 * tokens_at(off), 2)
        return remote(pair_out.at[chunks], pair_in.at[chunks], pair_s.at[off], pair_r.at[off], f, other)

    def backward(off):
        for k in range(1, n_f):
            share(k, off, peer(n_f - k)).wait_recv()
        tb = tokens_at(off)
        grads = jnp.concatenate([gp[tb, j] for j in range(3)], axis=0)

        def rows_for(n, core):
            rows = pl.ds(pl.multiple_of((4 * n + 2 * core) * BLOCK, 2 * BLOCK), 2 * BLOCK)
            return dot(wn[rows, :], grads, (1, 0))

        for n in range(2):
            pair_out[2 * tb + n] = rows_for(n, 1 - c).astype(jnp.bfloat16)
        start(pair(off))
        for n in range(2):
            own[2 * tb + n] = rows_for(n, c)

    def pass_on(way, step, half):
        return remote(
            ring_out.at[way, step, half], ring_in.at[way, step, half],
            sum_s.at[way, step, half], sum_r.at[way, step, half], f, up if way == UP else down,
        )

    def local(slot, half):
        rows = slice(half * BLOCK, (half + 1) * BLOCK)
        return own[slot, rows, :] + pair_in[slot, rows, :].astype(jnp.float32)

    for off in needed[0]:
        backward(off)
    for step in range(half_z):
        for off in needed[step]:
            pair(off).wait_recv()
        for way in (UP, DOWN):
            if step < hops[way]:
                slot = along(half_z - step if way == UP else step - hops[DOWN])
                for half in range(2):
                    total = local(slot, half)
                    if step > 0:
                        pass_on(way, step - 1, half).wait_recv()
                        total = total + ring_in[way, step - 1, half].astype(jnp.float32)
                    ring_out[way, step, half] = total.astype(jnp.bfloat16)
                    start(pass_on(way, step, half))
        if step == 0:
            for k in range(1, n_f):
                start(share_filter(k, f))
        if step + 1 < half_z:
            for off in needed[step + 1]:
                backward(off)

    for half in range(2):
        total = local(z, half)
        for way in (UP, DOWN):
            pass_on(way, hops[way] - 1, half).wait_recv()
            total = total + ring_in[way, hops[way] - 1, half].astype(jnp.float32)
        last_out[half] = total.astype(jnp.bfloat16)
        start(remote(
            last_out.at[half], last_in.at[xh], last_s.at[half], last_r.at[xh], from_f, from_m(half)
        ))
    for k in range(1, n_f):
        share_filter(k, peer(n_f - k)).wait_recv()
    filter_grad[...] = jnp.concatenate([fg_all[g, 0:1, :] for g in range(n_f)], axis=0)
    for x in range(2):
        remote(last_out.at[x], last_in.at[x], last_s.at[x], last_r.at[x], to_f, to_m(x)).wait_recv()
    summed = last_in[0].astype(jnp.float32) + last_in[1].astype(jnp.float32)
    input_grad[...] = summed.T.astype(jnp.bfloat16)
    for copy in sent:
        copy.wait_send()


def on_device(n_f, n_z, tokens, in_values, in_scales, filters, out_weight, cotangent):
    channels = in_values.shape[2]
    features = PIECES * BLOCK
    bf16, f32 = jnp.bfloat16, jnp.float32
    dma = pltpu.SemaphoreType.DMA
    values, scales = in_values.transpose(1, 0, 2), in_scales.transpose(1, 0, 2)
    return pl.pallas_call(
        functools.partial(kernel, n_f, n_z),
        out_shape=(
            jax.ShapeDtypeStruct((BLOCK, BLOCK), bf16),
            jax.ShapeDtypeStruct((n_f, BLOCK), f32),
        ),
        in_specs=[pl.BlockSpec(memory_space=pl.ANY)] * 6,
        out_specs=(pl.BlockSpec(memory_space=pltpu.VMEM),) * 2,
        scratch_shapes=[
            pltpu.VMEM(values.shape, bf16),
            pltpu.VMEM(scales.shape, bf16),
            pltpu.VMEM(filters.shape, f32),
            pltpu.VMEM(out_weight.shape, bf16),
            pltpu.VMEM((n_z, 2, 2, 2, BLOCK, BLOCK), bf16),
            pltpu.VMEM((3 * channels, features), bf16),
            pltpu.VMEM((features, 3 * channels), bf16),
            pltpu.VMEM((channels, features), bf16),
            pltpu.VMEM((n_f, 4, channels, BLOCK), bf16),
            pltpu.VMEM((n_f - 1, n_f, 4, GROUP, BLOCK), bf16),
            pltpu.VMEM((n_f, 3, channels, BLOCK), bf16),
            pltpu.VMEM((n_f, 8, BLOCK), f32),
            pltpu.VMEM((n_z, 2 * BLOCK, BLOCK), f32),
            pltpu.VMEM((n_z, 2 * BLOCK, BLOCK), bf16),
            pltpu.VMEM((n_z, 2 * BLOCK, BLOCK), bf16),
            pltpu.VMEM((2, n_z // 2, 2, BLOCK, BLOCK), bf16),
            pltpu.VMEM((2, n_z // 2, 2, BLOCK, BLOCK), bf16),
            pltpu.VMEM((2, BLOCK, BLOCK), bf16),
            pltpu.VMEM((2, BLOCK, BLOCK), bf16),
            dma((4,)),
            dma((2,)), dma((2,)),
            dma((3, 2, n_z // 2)), dma((3, 2, n_z // 2)),
            dma((n_z + 1,)), dma((n_z + 1,)),
            dma((2, n_z)), dma((2, n_z)),
            dma((n_f - 1, n_f)), dma((n_f - 1, n_f)),
            dma((n_f - 1, n_f)), dma((n_f - 1, n_f)),
            dma((n_f - 1,)), dma((n_f - 1,)),
            dma((n_f,)), dma((n_f,)),
            dma((2, n_z // 2, 2)), dma((2, n_z // 2, 2)),
            dma((2,)), dma((2,)),
        ],
        compiler_params=pltpu.CompilerParams(
            collective_id=0, has_side_effects=True, vmem_limit_bytes=56 << 20
        ),
        name="hyena",
    )(tokens, cotangent, values, scales, filters, out_weight)


def solution(mesh):
    placed = (
        P("fsdp", "tensor"),
        P("fsdp", None, "tensor"),
        P("fsdp", None, "tensor"),
        P("tensor", None),
        P("tensor", "fsdp"),
        P("fsdp", "tensor"),
    )
    return jax.shard_map(
        functools.partial(on_device, mesh.shape["fsdp"], mesh.shape["tensor"] // 4),
        mesh=mesh,
        in_specs=placed,
        out_specs=(P("fsdp", "tensor"), P("tensor", None)),
        check_vma=False,
    )
```

```python
import functools

import jax
import jax.numpy as jnp
from jax import lax
from jax.experimental import pallas as pl
from jax.experimental.pallas import tpu as pltpu
from jax.sharding import PartitionSpec as P

MESH = pl.DeviceIdType.MESH
BLOCK = 128
GROUP = 16
PIECES = 8
UP, DOWN = 0, 1


def piece_at(position):
    odd_node, core, half = position // 4, (position // 2) % 2, position % 2
    return 4 * odd_node + 2 * half + 1 - core


def dot(a, b, contract, precision=None):
    return lax.dot_general(
        a, b, ((contract[:1], contract[1:]), ((), ())),
        preferred_element_type=jnp.float32, precision=precision,
    )


def exact(a, b, contract):
    return dot(a, b, contract, lax.Precision.HIGHEST)


def kernel(
    n_f, n_z,
    tok, cot, val_hbm, scl_hbm, flt_hbm, out_w_hbm,
    input_grad, filter_grad,
    val, scl, flt, out_w, gathered, wt, wn, ow, part, part_in, gp, fg_all,
    own, pair_out, pair_in, ring_out, ring_in, last_out, last_in,
    in_s, perm_s, perm_r, ring_s, ring_r, slice_s, slice_r, core_s, core_r, rs_s, rs_r, ag_s, ag_r, fg_s, fg_r,
    pair_s, pair_r, sum_s, sum_r, last_s, last_r,
):
    channels = val.shape[2]
    half_z, half_f = n_z // 2, n_f // 2
    f, m = lax.axis_index("fsdp"), lax.axis_index("tensor")
    c, z, xh = lax.rem(m, 2), lax.rem(m // 2, n_z), m // (2 * n_z)
    along = lambda by: lax.rem(z + by + 2 * n_z, n_z)
    node = lambda by: (xh * n_z + along(by)) * 2 + c
    up, down = node(1), node(-1)
    other = m + 1 - 2 * c
    across_x = ((1 - xh) * n_z + z) * 2 + c
    peer = lambda k: lax.rem(f + k, n_f)
    tokens_at = lambda off: lax.rem(z // 2 + off + n_f, n_f)

    jm = lax.rem(m, PIECES)
    to_f, to_z, to_c, to_half = m // PIECES, 2 * f + jm // 4, 1 - lax.rem(jm, 2), lax.rem(jm, 4) // 2
    to_m = lambda x: (x * n_z + to_z) * 2 + to_c
    from_f = z // 2
    from_m = lambda half: PIECES * f + 4 * lax.rem(z, 2) + 2 * half + 1 - c

    def parent(d):
        if d % 3 < 2:
            return d - 3 if d % 3 == 0 else d - 1
        return d + 1 if d < half_z else d - 2

    reach = sorted({abs(d - parent(d)) for d in range(1, half_z + 1)})

    def remote(src, dst, send, recv, fsdp, tensor):
        return pltpu.make_async_remote_copy(
            src_ref=src, dst_ref=dst, send_sem=send, recv_sem=recv,
            device_id={"fsdp": fsdp, "tensor": tensor}, device_id_type=MESH,
        )

    sent = []

    def start(copy):
        copy.start()
        sent.append(copy)

    loads = [
        pltpu.make_async_copy(src, dst, in_s.at[i])
        for i, (src, dst) in enumerate(
            ((val_hbm, val), (scl_hbm, scl), (flt_hbm, flt), (out_w_hbm, out_w))
        )
    ]
    for load in loads:
        load.start()
    barrier = pltpu.get_barrier_semaphore()
    greeted = [(f, other), (f, across_x)] + [(f, node(way * by)) for by in reach for way in (1, -1)]
    greeted += [(peer(k), m) for k in range(1, n_f)]
    greeted += [(to_f, to_m(x)) for x in range(2)]
    greeted += [(from_f, from_m(h)) for h in range(2)]
    for fsdp, tensor in greeted:
        pl.semaphore_signal(
            barrier, inc=1, device_id={"fsdp": fsdp, "tensor": tensor}, device_id_type=MESH
        )
    pl.semaphore_wait(barrier, len(greeted))

    for a, block in enumerate((tok, cot)):
        start(remote(
            block, gathered.at[to_z, to_c, to_half, a], perm_s.at[a], perm_r.at[a], to_f, to_m(to_half)
        ))

    for load in loads:
        load.wait()
    for position in range(PIECES):
        piece = piece_at(position)
        rows = slice(position * BLOCK, (position + 1) * BLOCK)
        for j in range(3):
            scaled = val[j, piece * BLOCK : (piece + 1) * BLOCK, :].astype(jnp.float32) * scl[
                j, piece : piece + 1, :
            ].astype(jnp.float32)
            columns = slice(j * channels, (j + 1) * channels)
            wn[rows, columns] = scaled.astype(jnp.bfloat16)
            wt[columns, rows] = scaled.T.astype(jnp.bfloat16)
        ow[:, rows] = out_w[:, piece * BLOCK : (piece + 1) * BLOCK]

    steps = ((half_z, half_z - 1), (half_z - 1, half_z), (half_z, half_z - 1))

    chains = ((0, xh), (1, xh), (0, 1 - xh))

    def ring(chain, way, step, ahead=0):
        slot = along(-step - ahead if way == UP else step + ahead)
        a, half = chains[chain]
        chunk = gathered.at[slot, c, half, a]
        return remote(
            chunk, chunk, ring_s.at[chain, way, step], ring_r.at[chain, way, step],
            f, up if way == UP else down,
        )

    def over_x(by, half):
        chunk = gathered.at[along(by), c, half, 1]
        return remote(chunk, chunk, slice_s.at[by % n_z], slice_r.at[by % n_z], f, across_x)

    def first_over_x(half):
        chunk = gathered.at[z, c, half, 0]
        return remote(chunk, chunk, slice_s.at[n_z], slice_r.at[n_z], f, across_x)

    def over_core(by, half, which, core):
        chunk = gathered.at[along(by), core, half]
        return remote(chunk, chunk, core_s.at[which, by % n_z], core_r.at[which, by % n_z], f, other)

    def nodes_at(distance):
        return [distance] if distance in (0, half_z) else [-distance, distance]

    def rows_of(tb, a):
        blocks = [gathered[2 * tb + n, core, half, a] for n in range(2) for core in range(2) for half in range(2)]
        return jnp.concatenate(blocks, axis=1)

    group_rows = lambda g: pl.ds(pl.multiple_of(g * GROUP, GROUP), GROUP)

    def scatter(k, off):
        return remote(
            part.at[tokens_at(off), :, group_rows(peer(k)), :], part_in.at[k - 1, tokens_at(off)],
            rs_s.at[k - 1, off % n_f], rs_r.at[k - 1, off % n_f], peer(k), m,
        )

    def products(distance):
        for d in (2 * distance, 2 * distance + 1):
            if d <= half_z:
                for by in nodes_at(d):
                    over_core(by, xh, 0, 1 - c).wait_recv()
                    over_core(by, 1 - xh, 1, 1 - c).wait_recv()
        for off in [distance] if distance in (0, half_f) else [-distance, distance]:
            tb = tokens_at(off)
            proj = dot(wt[...], rows_of(tb, 0), (1, 1)).astype(jnp.bfloat16)
            for j in range(3):
                part[tb, j] = proj[j * channels : (j + 1) * channels]
            part[tb, 3] = dot(ow[...], rows_of(tb, 1), (1, 1)).astype(jnp.bfloat16)
            for k in range(1, n_f):
                start(scatter(k, off))

    def arrived(chain, step):
        for way in (UP, DOWN):
            if step < steps[chain][way]:
                ring(chain, way, step, 1).wait_recv()
                if step + 1 < steps[chain][way]:
                    start(ring(chain, way, step + 1))

    for a in range(2):
        block = gathered.at[z, c, xh, a]
        remote(block, block, perm_s.at[a], perm_r.at[a], f, other).wait_recv()
        if a == 0:
            start(first_over_x(xh))
        for way in (UP, DOWN):
            start(ring(a, way, 0))
    start(over_x(0, xh))
    start(over_core(0, xh, 0, c))
    done = 0
    for step in range(half_z + 2):
        if step < half_z:
            for chain in range(2):
                arrived(chain, step)
            for by in nodes_at(step + 1):
                start(over_x(by, xh))
        if step == 0:
            first_over_x(1 - xh).wait_recv()
            for way in (UP, DOWN):
                start(ring(2, way, 0))
        if step >= 1:
            if step - 1 < half_z:
                arrived(2, step - 1)
            for by in nodes_at(step - 1):
                over_x(by, 1 - xh).wait_recv()
                start(over_core(by, 1 - xh, 1, c))
        if step < half_z:
            for by in nodes_at(step + 1):
                start(over_core(by, xh, 0, c))
        if step >= 2 * done + 3 and done < half_f:
            products(done)
            done += 1
    for distance in range(done, half_f + 1):
        products(distance)

    mine = group_rows(f)
    offsets = [off for d in range(half_f + 1) for off in ([d] if d in (0, half_f) else [-d, d])]
    taps = jnp.concatenate([flt[pl.ds(f, 1), :], jnp.zeros((1, BLOCK), jnp.float32)], axis=1)
    band = pltpu.roll(jnp.broadcast_to(taps, (BLOCK, 2 * BLOCK)), 0, 1, stride=1, stride_axis=0)
    band_here, band_next = band[:, :BLOCK], band[:, BLOCK:]
    for off in offsets:
        for k in range(1, n_f):
            scatter(k, off).wait_recv()

    def summed_part(j):
        total = part[:, j, mine, :].astype(jnp.float32)
        for k in range(1, n_f):
            total = total + part_in[k - 1, :, j].astype(jnp.float32)
        return total.reshape(n_f * GROUP, BLOCK)

    query, key, value = (
        summed_part(j).astype(jnp.bfloat16).astype(jnp.float32) for j in range(3)
    )
    grad_z = summed_part(3)
    nothing = jnp.zeros((GROUP, BLOCK), jnp.float32)
    product = key * value
    before = jnp.concatenate([nothing, product[:-GROUP]], axis=0)
    conv = exact(product, band_here, (1, 0)) + exact(before, band_next, (1, 0))
    grad_query = grad_z * conv
    grad_conv = grad_z * query
    after = jnp.concatenate([grad_conv[GROUP:], nothing], axis=0)
    grad_product = exact(grad_conv, band_here, (1, 1)) + exact(after, band_next, (1, 1))
    for j, grad in enumerate((grad_query, grad_product * value, grad_product * key)):
        gp[:, j, mine, :] = grad.astype(jnp.bfloat16).reshape(n_f, GROUP, BLOCK)

    tree = [d for d in (8, 7, 5, 4, 2, 6, 1, 3) if d <= half_z]
    needed = {}
    for d in tree + [0]:
        needed[d] = []
        for off in [((odd + by) // 2) % n_f for by in nodes_at(d) for odd in range(2)]:
            if off not in needed[d] and all(off not in seen for seen in needed.values()):
                needed[d].append(off)

    def share(k, off, owner):
        rows = gp.at[tokens_at(off), :, group_rows(owner), :]
        return remote(rows, rows, ag_s.at[k - 1, off], ag_r.at[k - 1, off], peer(k), m)

    for fresh in needed.values():
        for off in fresh:
            for k in range(1, n_f):
                start(share(k, off, f))

    flip = (
        lax.broadcasted_iota(jnp.int32, (BLOCK, BLOCK), 0)
        + lax.broadcasted_iota(jnp.int32, (BLOCK, BLOCK), 1)
        == BLOCK - 1
    ).astype(jnp.float32)
    turned = exact(product, flip, (1, 0))
    corr = exact(turned, jnp.concatenate([grad_conv, after], axis=1), (0, 0))
    skewed = pltpu.roll(corr, 0, 1, stride=1, stride_axis=0)
    lags = pltpu.roll(jnp.sum(skewed, axis=0, keepdims=True), BLOCK + 1, 1)[:, :BLOCK]
    fg_all[f] = jnp.broadcast_to(lags * (1.0 / BLOCK), (8, BLOCK))

    def share_filter(k, owner):
        return remote(fg_all.at[owner], fg_all.at[owner], fg_s.at[k - 1], fg_r.at[k - 1], peer(k), m)

    def pair(off):
        chunks = pl.ds(2 * tokens_at(off), 2)
        return remote(pair_out.at[chunks], pair_in.at[chunks], pair_s.at[off], pair_r.at[off], f, other)

    def backward(off):
        for k in range(1, n_f):
            share(k, off, peer(n_f - k)).wait_recv()
        tb = tokens_at(off)
        grads = jnp.concatenate([gp[tb, j] for j in range(3)], axis=0)

        def rows_for(n, core):
            rows = pl.ds(pl.multiple_of((4 * n + 2 * core) * BLOCK, 2 * BLOCK), 2 * BLOCK)
            return dot(wn[rows, :], grads, (1, 0))

        for n in range(2):
            pair_out[2 * tb + n] = rows_for(n, 1 - c).astype(jnp.bfloat16)
        start(pair(off))
        for n in range(2):
            own[2 * tb + n] = rows_for(n, c)

    def taken(half, way, d):
        return d <= (half_z if (way == UP) == (half == 0) else half_z - 1)

    def pass_on(half, way, d):
        by = d - parent(d)
        return remote(
            ring_out.at[half, way, d - 1], ring_in.at[half, way, d - 1],
            sum_s.at[half, way, d - 1], sum_r.at[half, way, d - 1], f, node(by if way == UP else -by),
        )

    def with_children(total, half, way, at):
        for d in tree:
            if parent(d) == at and taken(half, way, d):
                pass_on(half, way, d).wait_recv()
                total = total + ring_in[half, way, d - 1].astype(jnp.float32)
        return total

    def local(slot, half):
        rows = slice(half * BLOCK, (half + 1) * BLOCK)
        return own[slot, rows, :] + pair_in[slot, rows, :].astype(jnp.float32)

    for i, d in enumerate(tree):
        for off in needed[d]:
            backward(off)
        for off in needed[d]:
            pair(off).wait_recv()
        for way in (UP, DOWN):
            slot = along(d if way == UP else -d)
            for half in range(2):
                if taken(half, way, d):
                    ring_out[half, way, d - 1] = with_children(local(slot, half), half, way, d).astype(jnp.bfloat16)
                    start(pass_on(half, way, d))
        if i == 0:
            for k in range(1, n_f):
                start(share_filter(k, f))
    for off in needed[0]:
        backward(off)
        pair(off).wait_recv()

    for half in range(2):
        total = local(z, half)
        for way in (UP, DOWN):
            total = with_children(total, half, way, 0)
        last_out[half] = total.astype(jnp.bfloat16)
        start(remote(
            last_out.at[half], last_in.at[xh], last_s.at[half], last_r.at[xh], from_f, from_m(half)
        ))
    for k in range(1, n_f):
        share_filter(k, peer(n_f - k)).wait_recv()
    filter_grad[...] = jnp.concatenate([fg_all[g, 0:1, :] for g in range(n_f)], axis=0)
    for x in range(2):
        remote(last_out.at[x], last_in.at[x], last_s.at[x], last_r.at[x], to_f, to_m(x)).wait_recv()
    summed = last_in[0].astype(jnp.float32) + last_in[1].astype(jnp.float32)
    input_grad[...] = summed.T.astype(jnp.bfloat16)
    for copy in sent:
        copy.wait_send()


def on_device(n_f, n_z, tokens, in_values, in_scales, filters, out_weight, cotangent):
    channels = in_values.shape[2]
    features = PIECES * BLOCK
    bf16, f32 = jnp.bfloat16, jnp.float32
    dma = pltpu.SemaphoreType.DMA
    values, scales = in_values.transpose(1, 0, 2), in_scales.transpose(1, 0, 2)
    return pl.pallas_call(
        functools.partial(kernel, n_f, n_z),
        out_shape=(
            jax.ShapeDtypeStruct((BLOCK, BLOCK), bf16),
            jax.ShapeDtypeStruct((n_f, BLOCK), f32),
        ),
        in_specs=[pl.BlockSpec(memory_space=pl.ANY)] * 6,
        out_specs=(pl.BlockSpec(memory_space=pltpu.VMEM),) * 2,
        scratch_shapes=[
            pltpu.VMEM(values.shape, bf16),
            pltpu.VMEM(scales.shape, bf16),
            pltpu.VMEM(filters.shape, f32),
            pltpu.VMEM(out_weight.shape, bf16),
            pltpu.VMEM((n_z, 2, 2, 2, BLOCK, BLOCK), bf16),
            pltpu.VMEM((3 * channels, features), bf16),
            pltpu.VMEM((features, 3 * channels), bf16),
            pltpu.VMEM((channels, features), bf16),
            pltpu.VMEM((n_f, 4, channels, BLOCK), bf16),
            pltpu.VMEM((n_f - 1, n_f, 4, GROUP, BLOCK), bf16),
            pltpu.VMEM((n_f, 3, channels, BLOCK), bf16),
            pltpu.VMEM((n_f, 8, BLOCK), f32),
            pltpu.VMEM((n_z, 2 * BLOCK, BLOCK), f32),
            pltpu.VMEM((n_z, 2 * BLOCK, BLOCK), bf16),
            pltpu.VMEM((n_z, 2 * BLOCK, BLOCK), bf16),
            pltpu.VMEM((2, 2, n_z // 2, BLOCK, BLOCK), bf16),
            pltpu.VMEM((2, 2, n_z // 2, BLOCK, BLOCK), bf16),
            pltpu.VMEM((2, BLOCK, BLOCK), bf16),
            pltpu.VMEM((2, BLOCK, BLOCK), bf16),
            dma((4,)),
            dma((2,)), dma((2,)),
            dma((3, 2, n_z // 2)), dma((3, 2, n_z // 2)),
            dma((n_z + 1,)), dma((n_z + 1,)),
            dma((2, n_z)), dma((2, n_z)),
            dma((n_f - 1, n_f)), dma((n_f - 1, n_f)),
            dma((n_f - 1, n_f)), dma((n_f - 1, n_f)),
            dma((n_f - 1,)), dma((n_f - 1,)),
            dma((n_f,)), dma((n_f,)),
            dma((2, 2, n_z // 2)), dma((2, 2, n_z // 2)),
            dma((2,)), dma((2,)),
        ],
        compiler_params=pltpu.CompilerParams(
            collective_id=0, has_side_effects=True, vmem_limit_bytes=56 << 20
        ),
        name="hyena",
    )(tokens, cotangent, values, scales, filters, out_weight)


def solution(mesh):
    placed = (
        P("fsdp", "tensor"),
        P("fsdp", None, "tensor"),
        P("fsdp", None, "tensor"),
        P("tensor", None),
        P("tensor", "fsdp"),
        P("fsdp", "tensor"),
    )
    return jax.shard_map(
        functools.partial(on_device, mesh.shape["fsdp"], mesh.shape["tensor"] // 4),
        mesh=mesh,
        in_specs=placed,
        out_specs=(P("fsdp", "tensor"), P("tensor", None)),
        check_vma=False,
    )
```

```python
import functools

import jax
import jax.numpy as jnp
from jax import lax
from jax.experimental import pallas as pl
from jax.experimental.pallas import tpu as pltpu
from jax.sharding import PartitionSpec as P

MESH = pl.DeviceIdType.MESH
BLOCK = 128
GROUP = 16
PIECES = 8
UP, DOWN = 0, 1


def piece_at(position):
    odd_node, core, half = position // 4, (position // 2) % 2, position % 2
    return 4 * odd_node + 2 * half + 1 - core


def dot(a, b, contract, precision=None):
    return lax.dot_general(
        a, b, ((contract[:1], contract[1:]), ((), ())),
        preferred_element_type=jnp.float32, precision=precision,
    )


def exact(a, b, contract):
    return dot(a, b, contract, lax.Precision.HIGHEST)


def kernel(
    n_f, n_z,
    tok, cot, val_hbm, scl_hbm, flt_hbm, out_w_hbm,
    input_grad, filter_grad,
    val, scl, flt, out_w, gathered, wt, wn, ow, part, part_in, gp, fg_all,
    own, pair_out, pair_in, ring_out, ring_in, last_out, last_in,
    in_s, perm_s, perm_r, ring_s, ring_r, slice_s, slice_r, core_s, core_r, rs_s, rs_r, ag_s, ag_r, fg_s, fg_r,
    pair_s, pair_r, sum_s, sum_r, last_s, last_r,
):
    channels = val.shape[2]
    half_z, half_f = n_z // 2, n_f // 2
    f, m = lax.axis_index("fsdp"), lax.axis_index("tensor")
    c, z, xh = lax.rem(m, 2), lax.rem(m // 2, n_z), m // (2 * n_z)
    along = lambda by: lax.rem(z + by + 2 * n_z, n_z)
    node = lambda by: (xh * n_z + along(by)) * 2 + c
    up, down = node(1), node(-1)
    other = m + 1 - 2 * c
    across_x = ((1 - xh) * n_z + z) * 2 + c
    peer = lambda k: lax.rem(f + k, n_f)
    tokens_at = lambda off: lax.rem(z // 2 + off + n_f, n_f)

    jm = lax.rem(m, PIECES)
    to_f, to_z, to_c, to_half = m // PIECES, 2 * f + jm // 4, 1 - lax.rem(jm, 2), lax.rem(jm, 4) // 2
    to_m = lambda x: (x * n_z + to_z) * 2 + to_c
    from_f = z // 2
    from_m = lambda half: PIECES * f + 4 * lax.rem(z, 2) + 2 * half + 1 - c

    def parent(d):
        if d % 3 < 2:
            return d - 3 if d % 3 == 0 else d - 1
        return d + 1 if d < half_z else d - 2

    reach = sorted({abs(d - parent(d)) for d in range(1, half_z + 1)})

    def remote(src, dst, send, recv, fsdp, tensor):
        return pltpu.make_async_remote_copy(
            src_ref=src, dst_ref=dst, send_sem=send, recv_sem=recv,
            device_id={"fsdp": fsdp, "tensor": tensor}, device_id_type=MESH,
        )

    sent = []

    def start(copy):
        copy.start()
        sent.append(copy)

    loads = [
        pltpu.make_async_copy(src, dst, in_s.at[i])
        for i, (src, dst) in enumerate(
            ((val_hbm, val), (scl_hbm, scl), (flt_hbm, flt), (out_w_hbm, out_w))
        )
    ]
    for load in loads:
        load.start()
    barrier = pltpu.get_barrier_semaphore()
    greeted = [(f, other), (f, across_x)] + [(f, node(way * by)) for by in reach for way in (1, -1)]
    greeted += [(peer(k), m) for k in range(1, n_f)]
    greeted += [(to_f, to_m(x)) for x in range(2)]
    greeted += [(from_f, from_m(h)) for h in range(2)]
    for fsdp, tensor in greeted:
        pl.semaphore_signal(
            barrier, inc=1, device_id={"fsdp": fsdp, "tensor": tensor}, device_id_type=MESH
        )
    pl.semaphore_wait(barrier, len(greeted))

    for a, block in enumerate((tok, cot)):
        start(remote(
            block, gathered.at[to_z, to_c, to_half, a], perm_s.at[a], perm_r.at[a], to_f, to_m(to_half)
        ))

    for load in loads:
        load.wait()
    for position in range(PIECES):
        piece = piece_at(position)
        rows = slice(position * BLOCK, (position + 1) * BLOCK)
        for j in range(3):
            scaled = val[j, piece * BLOCK : (piece + 1) * BLOCK, :].astype(jnp.float32) * scl[
                j, piece : piece + 1, :
            ].astype(jnp.float32)
            columns = slice(j * channels, (j + 1) * channels)
            wn[rows, columns] = scaled.astype(jnp.bfloat16)
            wt[columns, rows] = scaled.T.astype(jnp.bfloat16)
        ow[:, rows] = out_w[:, piece * BLOCK : (piece + 1) * BLOCK]

    steps = ((half_z, half_z - 1), (half_z - 1, half_z), (half_z, half_z - 1))

    chains = ((0, xh), (1, xh), (0, 1 - xh))

    def ring(chain, way, step, ahead=0):
        slot = along(-step - ahead if way == UP else step + ahead)
        a, half = chains[chain]
        chunk = gathered.at[slot, c, half, a]
        return remote(
            chunk, chunk, ring_s.at[chain, way, step], ring_r.at[chain, way, step],
            f, up if way == UP else down,
        )

    def over_x(by, half):
        chunk = gathered.at[along(by), c, half, 1]
        return remote(chunk, chunk, slice_s.at[by % n_z], slice_r.at[by % n_z], f, across_x)

    def first_over_x(half):
        chunk = gathered.at[z, c, half, 0]
        return remote(chunk, chunk, slice_s.at[n_z], slice_r.at[n_z], f, across_x)

    def over_core(by, half, which, core):
        chunk = gathered.at[along(by), core, half]
        return remote(chunk, chunk, core_s.at[which, by % n_z], core_r.at[which, by % n_z], f, other)

    def nodes_at(distance):
        return [distance] if distance in (0, half_z) else [-distance, distance]

    def rows_of(tb, a):
        blocks = [gathered[2 * tb + n, core, half, a] for n in range(2) for core in range(2) for half in range(2)]
        return jnp.concatenate(blocks, axis=1)

    group_rows = lambda g: pl.ds(pl.multiple_of(g * GROUP, GROUP), GROUP)

    def scatter(k, off):
        return remote(
            part.at[tokens_at(off), :, group_rows(peer(k)), :], part_in.at[k - 1, tokens_at(off)],
            rs_s.at[k - 1, off % n_f], rs_r.at[k - 1, off % n_f], peer(k), m,
        )

    def products(distance):
        for d in (2 * distance, 2 * distance + 1):
            if d <= half_z:
                for by in nodes_at(d):
                    over_core(by, xh, 0, 1 - c).wait_recv()
                    over_core(by, 1 - xh, 1, 1 - c).wait_recv()
        for off in [distance] if distance in (0, half_f) else [-distance, distance]:
            tb = tokens_at(off)
            proj = dot(wt[...], rows_of(tb, 0), (1, 1)).astype(jnp.bfloat16)
            for j in range(3):
                part[tb, j] = proj[j * channels : (j + 1) * channels]
            part[tb, 3] = dot(ow[...], rows_of(tb, 1), (1, 1)).astype(jnp.bfloat16)
            for k in range(1, n_f):
                start(scatter(k, off))

    def arrived(chain, step):
        for way in (UP, DOWN):
            if step < steps[chain][way]:
                ring(chain, way, step, 1).wait_recv()
                if step + 1 < steps[chain][way]:
                    start(ring(chain, way, step + 1))

    for a in range(2):
        block = gathered.at[z, c, xh, a]
        remote(block, block, perm_s.at[a], perm_r.at[a], f, other).wait_recv()
        if a == 0:
            start(first_over_x(xh))
        for way in (UP, DOWN):
            start(ring(a, way, 0))
    start(over_x(0, xh))
    start(over_core(0, xh, 0, c))
    done = 0
    for step in range(half_z + 2):
        if step < half_z:
            for chain in range(2):
                arrived(chain, step)
            for by in nodes_at(step + 1):
                start(over_x(by, xh))
        if step == 0:
            first_over_x(1 - xh).wait_recv()
            for way in (UP, DOWN):
                start(ring(2, way, 0))
        if step >= 1:
            if step - 1 < half_z:
                arrived(2, step - 1)
            for by in nodes_at(step - 1):
                over_x(by, 1 - xh).wait_recv()
                start(over_core(by, 1 - xh, 1, c))
        if step < half_z:
            for by in nodes_at(step + 1):
                start(over_core(by, xh, 0, c))
        if step >= 2 * done + 3 and done < half_f:
            products(done)
            done += 1
    for distance in range(done, half_f + 1):
        products(distance)

    mine = group_rows(f)
    offsets = [off for d in range(half_f + 1) for off in ([d] if d in (0, half_f) else [-d, d])]
    taps = jnp.concatenate([flt[pl.ds(f, 1), :], jnp.zeros((1, BLOCK), jnp.float32)], axis=1)
    band = pltpu.roll(jnp.broadcast_to(taps, (BLOCK, 2 * BLOCK)), 0, 1, stride=1, stride_axis=0)
    band_here, band_next = band[:, :BLOCK], band[:, BLOCK:]
    for off in offsets:
        for k in range(1, n_f):
            scatter(k, off).wait_recv()

    def summed_part(j):
        total = part[:, j, mine, :].astype(jnp.float32)
        for k in range(1, n_f):
            total = total + part_in[k - 1, :, j].astype(jnp.float32)
        return total.reshape(n_f * GROUP, BLOCK)

    query, key, value = (
        summed_part(j).astype(jnp.bfloat16).astype(jnp.float32) for j in range(3)
    )
    grad_z = summed_part(3)
    nothing = jnp.zeros((GROUP, BLOCK), jnp.float32)
    product = key * value
    before = jnp.concatenate([nothing, product[:-GROUP]], axis=0)
    conv = exact(product, band_here, (1, 0)) + exact(before, band_next, (1, 0))
    grad_query = grad_z * conv
    grad_conv = grad_z * query
    after = jnp.concatenate([grad_conv[GROUP:], nothing], axis=0)
    grad_product = exact(grad_conv, band_here, (1, 1)) + exact(after, band_next, (1, 1))
    for j, grad in enumerate((grad_query, grad_product * value, grad_product * key)):
        gp[:, j, mine, :] = grad.astype(jnp.bfloat16).reshape(n_f, GROUP, BLOCK)

    tree = [d for d in (8, 7, 5, 4, 2, 6, 1, 3) if d <= half_z]
    needed = {}
    for d in tree + [0]:
        needed[d] = []
        for off in [((odd + by) // 2) % n_f for by in nodes_at(d) for odd in range(2)]:
            if off not in needed[d] and all(off not in seen for seen in needed.values()):
                needed[d].append(off)

    def share(k, off, owner):
        rows = gp.at[tokens_at(off), :, group_rows(owner), :]
        return remote(rows, rows, ag_s.at[k - 1, off], ag_r.at[k - 1, off], peer(k), m)

    for fresh in needed.values():
        for off in fresh:
            for k in range(1, n_f):
                start(share(k, off, f))

    flip = (
        lax.broadcasted_iota(jnp.int32, (BLOCK, BLOCK), 0)
        + lax.broadcasted_iota(jnp.int32, (BLOCK, BLOCK), 1)
        == BLOCK - 1
    ).astype(jnp.float32)
    turned = exact(product, flip, (1, 0))
    corr = exact(turned, jnp.concatenate([grad_conv, after], axis=1), (0, 0))
    skewed = pltpu.roll(corr, 0, 1, stride=1, stride_axis=0)
    lags = pltpu.roll(jnp.sum(skewed, axis=0, keepdims=True), BLOCK + 1, 1)[:, :BLOCK]
    fg_all[f] = jnp.broadcast_to(lags * (1.0 / BLOCK), (8, BLOCK))

    def share_filter(k, owner):
        return remote(fg_all.at[owner], fg_all.at[owner], fg_s.at[k - 1], fg_r.at[k - 1], peer(k), m)

    def pair(off):
        chunks = pl.ds(2 * tokens_at(off), 2)
        return remote(pair_out.at[chunks], pair_in.at[chunks], pair_s.at[off], pair_r.at[off], f, other)

    def backward(off):
        for k in range(1, n_f):
            share(k, off, peer(n_f - k)).wait_recv()
        tb = tokens_at(off)
        grads = jnp.concatenate([gp[tb, j] for j in range(3)], axis=0)

        def rows_for(n, core):
            rows = pl.ds(pl.multiple_of((4 * n + 2 * core) * BLOCK, 2 * BLOCK), 2 * BLOCK)
            return dot(wn[rows, :], grads, (1, 0))

        for n in range(2):
            pair_out[2 * tb + n] = rows_for(n, 1 - c).astype(jnp.bfloat16)
        start(pair(off))
        for n in range(2):
            own[2 * tb + n] = rows_for(n, c)

    def taken(half, way, d):
        return d <= (half_z if (way == UP) == (half == 0) else half_z - 1)

    def pass_on(half, way, d):
        by = d - parent(d)
        return remote(
            ring_out.at[half, way, d - 1], ring_in.at[half, way, d - 1],
            sum_s.at[half, way, d - 1], sum_r.at[half, way, d - 1], f, node(by if way == UP else -by),
        )

    def with_children(total, half, way, at):
        for d in tree:
            if parent(d) == at and taken(half, way, d):
                pass_on(half, way, d).wait_recv()
                total = total + ring_in[half, way, d - 1].astype(jnp.float32)
        return total

    def local(slot, half):
        rows = slice(half * BLOCK, (half + 1) * BLOCK)
        return own[slot, rows, :] + pair_in[slot, rows, :].astype(jnp.float32)

    for i, d in enumerate(tree):
        for off in needed[d]:
            backward(off)
        for off in needed[d]:
            pair(off).wait_recv()
        for way in (UP, DOWN):
            slot = along(d if way == UP else -d)
            for half in range(2):
                if taken(half, way, d):
                    ring_out[half, way, d - 1] = with_children(local(slot, half), half, way, d).astype(jnp.bfloat16)
                    start(pass_on(half, way, d))
        if i == 0:
            for k in range(1, n_f):
                start(share_filter(k, f))
    for off in needed[0]:
        backward(off)
        pair(off).wait_recv()

    for half in range(2):
        total = local(z, half)
        for way in (UP, DOWN):
            total = with_children(total, half, way, 0)
        last_out[half] = total.astype(jnp.bfloat16)
        start(remote(
            last_out.at[half], last_in.at[xh], last_s.at[half], last_r.at[xh], from_f, from_m(half)
        ))
    for k in range(1, n_f):
        share_filter(k, peer(n_f - k)).wait_recv()
    filter_grad[...] = jnp.concatenate([fg_all[g, 0:1, :] for g in range(n_f)], axis=0)
    for copy in sent[:-2]:
        copy.wait_send()
    for x in range(2):
        remote(last_out.at[x], last_in.at[x], last_s.at[x], last_r.at[x], to_f, to_m(x)).wait_recv()
    summed = last_in[0].astype(jnp.float32) + last_in[1].astype(jnp.float32)
    input_grad[...] = summed.T.astype(jnp.bfloat16)
    for copy in sent[-2:]:
        copy.wait_send()


def on_device(n_f, n_z, tokens, in_values, in_scales, filters, out_weight, cotangent):
    channels = in_values.shape[2]
    features = PIECES * BLOCK
    bf16, f32 = jnp.bfloat16, jnp.float32
    dma = pltpu.SemaphoreType.DMA
    values, scales = in_values.transpose(1, 0, 2), in_scales.transpose(1, 0, 2)
    return pl.pallas_call(
        functools.partial(kernel, n_f, n_z),
        out_shape=(
            jax.ShapeDtypeStruct((BLOCK, BLOCK), bf16),
            jax.ShapeDtypeStruct((n_f, BLOCK), f32),
        ),
        in_specs=[pl.BlockSpec(memory_space=pl.ANY)] * 6,
        out_specs=(pl.BlockSpec(memory_space=pltpu.VMEM),) * 2,
        scratch_shapes=[
            pltpu.VMEM(values.shape, bf16),
            pltpu.VMEM(scales.shape, bf16),
            pltpu.VMEM(filters.shape, f32),
            pltpu.VMEM(out_weight.shape, bf16),
            pltpu.VMEM((n_z, 2, 2, 2, BLOCK, BLOCK), bf16),
            pltpu.VMEM((3 * channels, features), bf16),
            pltpu.VMEM((features, 3 * channels), bf16),
            pltpu.VMEM((channels, features), bf16),
            pltpu.VMEM((n_f, 4, channels, BLOCK), bf16),
            pltpu.VMEM((n_f - 1, n_f, 4, GROUP, BLOCK), bf16),
            pltpu.VMEM((n_f, 3, channels, BLOCK), bf16),
            pltpu.VMEM((n_f, 8, BLOCK), f32),
            pltpu.VMEM((n_z, 2 * BLOCK, BLOCK), f32),
            pltpu.VMEM((n_z, 2 * BLOCK, BLOCK), bf16),
            pltpu.VMEM((n_z, 2 * BLOCK, BLOCK), bf16),
            pltpu.VMEM((2, 2, n_z // 2, BLOCK, BLOCK), bf16),
            pltpu.VMEM((2, 2, n_z // 2, BLOCK, BLOCK), bf16),
            pltpu.VMEM((2, BLOCK, BLOCK), bf16),
            pltpu.VMEM((2, BLOCK, BLOCK), bf16),
            dma((4,)),
            dma((2,)), dma((2,)),
            dma((3, 2, n_z // 2)), dma((3, 2, n_z // 2)),
            dma((n_z + 1,)), dma((n_z + 1,)),
            dma((2, n_z)), dma((2, n_z)),
            dma((n_f - 1, n_f)), dma((n_f - 1, n_f)),
            dma((n_f - 1, n_f)), dma((n_f - 1, n_f)),
            dma((n_f - 1,)), dma((n_f - 1,)),
            dma((n_f,)), dma((n_f,)),
            dma((2, 2, n_z // 2)), dma((2, 2, n_z // 2)),
            dma((2,)), dma((2,)),
        ],
        compiler_params=pltpu.CompilerParams(
            collective_id=0, has_side_effects=True, vmem_limit_bytes=56 << 20
        ),
        name="hyena",
    )(tokens, cotangent, values, scales, filters, out_weight)


def solution(mesh):
    placed = (
        P("fsdp", "tensor"),
        P("fsdp", None, "tensor"),
        P("fsdp", None, "tensor"),
        P("tensor", None),
        P("tensor", "fsdp"),
        P("fsdp", "tensor"),
    )
    return jax.shard_map(
        functools.partial(on_device, mesh.shape["fsdp"], mesh.shape["tensor"] // 4),
        mesh=mesh,
        in_specs=placed,
        out_specs=(P("fsdp", "tensor"), P("tensor", None)),
        check_vma=False,
    )
```

```python
import functools

import jax
import jax.numpy as jnp
from jax import lax
from jax.experimental import pallas as pl
from jax.experimental.pallas import tpu as pltpu
from jax.sharding import PartitionSpec as P

MESH = pl.DeviceIdType.MESH
BLOCK = 128
GROUP = 16
PIECES = 8
UP, DOWN = 0, 1


def piece_at(position):
    odd_node, core, half = position // 4, (position // 2) % 2, position % 2
    return 4 * odd_node + 2 * half + 1 - core


def dot(a, b, contract, precision=None):
    return lax.dot_general(
        a, b, ((contract[:1], contract[1:]), ((), ())),
        preferred_element_type=jnp.float32, precision=precision,
    )


def exact(a, b, contract):
    return dot(a, b, contract, lax.Precision.HIGHEST)


def kernel(
    n_f, n_z,
    tok, cot, val_hbm, scl_hbm, flt_hbm, out_w_hbm,
    input_grad, filter_grad,
    val, scl, flt, out_w, gathered, wt, wn, ow, part, part_in, gp, fg_all,
    own, pair_out, pair_in, ring_out, ring_in, last_out, last_in,
    in_s, perm_s, perm_r, ring_s, ring_r, slice_s, slice_r, core_s, core_r, rs_s, rs_r, ag_s, ag_r, fg_s, fg_r,
    pair_s, pair_r, sum_s, sum_r, last_s, last_r,
):
    channels = val.shape[2]
    half_z, half_f = n_z // 2, n_f // 2
    f, m = lax.axis_index("fsdp"), lax.axis_index("tensor")
    c, z, xh = lax.rem(m, 2), lax.rem(m // 2, n_z), m // (2 * n_z)
    along = lambda by: lax.rem(z + by + 2 * n_z, n_z)
    node = lambda by: (xh * n_z + along(by)) * 2 + c
    up, down = node(1), node(-1)
    other = m + 1 - 2 * c
    across_x = ((1 - xh) * n_z + z) * 2 + c
    peer = lambda k: lax.rem(f + k, n_f)
    tokens_at = lambda off: lax.rem(z // 2 + off + n_f, n_f)

    jm = lax.rem(m, PIECES)
    to_f, to_z, to_c, to_half = m // PIECES, 2 * f + jm // 4, 1 - lax.rem(jm, 2), lax.rem(jm, 4) // 2
    to_m = lambda x: (x * n_z + to_z) * 2 + to_c
    from_f = z // 2
    from_m = lambda half: PIECES * f + 4 * lax.rem(z, 2) + 2 * half + 1 - c

    def parent(d):
        if d % 3 < 2:
            return d - 3 if d % 3 == 0 else d - 1
        return d + 1 if d < half_z else d - 2

    reach = sorted({abs(d - parent(d)) for d in range(1, half_z + 1)})

    def remote(src, dst, send, recv, fsdp, tensor):
        return pltpu.make_async_remote_copy(
            src_ref=src, dst_ref=dst, send_sem=send, recv_sem=recv,
            device_id={"fsdp": fsdp, "tensor": tensor}, device_id_type=MESH,
        )

    sent = []

    def start(copy):
        copy.start()
        sent.append(copy)

    loads = [
        pltpu.make_async_copy(src, dst, in_s.at[i])
        for i, (src, dst) in enumerate(
            ((val_hbm, val), (scl_hbm, scl), (flt_hbm, flt), (out_w_hbm, out_w))
        )
    ]
    for load in loads:
        load.start()
    barrier = pltpu.get_barrier_semaphore()
    greeted = [(to_f, to_m(x)) for x in range(2)] + [(from_f, from_m(h)) for h in range(2)]
    greeted += [(peer(k), m) for k in range(1, n_f)]
    greeted += [(f, other), (f, across_x)] + [(f, node(way * by)) for by in reach for way in (1, -1)]
    for fsdp, tensor in greeted:
        pl.semaphore_signal(
            barrier, inc=1, device_id={"fsdp": fsdp, "tensor": tensor}, device_id_type=MESH
        )
    pl.semaphore_wait(barrier, len(greeted))

    for a, block in enumerate((tok, cot)):
        start(remote(
            block, gathered.at[to_z, to_c, to_half, a], perm_s.at[a], perm_r.at[a], to_f, to_m(to_half)
        ))

    for load in loads:
        load.wait()
    for position in range(PIECES):
        piece = piece_at(position)
        rows = slice(position * BLOCK, (position + 1) * BLOCK)
        for j in range(3):
            scaled = val[j, piece * BLOCK : (piece + 1) * BLOCK, :].astype(jnp.float32) * scl[
                j, piece : piece + 1, :
            ].astype(jnp.float32)
            columns = slice(j * channels, (j + 1) * channels)
            wn[rows, columns] = scaled.astype(jnp.bfloat16)
            wt[columns, rows] = scaled.T.astype(jnp.bfloat16)
        ow[:, rows] = out_w[:, piece * BLOCK : (piece + 1) * BLOCK]

    steps = ((half_z, half_z - 1), (half_z - 1, half_z), (half_z, half_z - 1))

    chains = ((0, xh), (1, xh), (0, 1 - xh))

    def ring(chain, way, step, ahead=0):
        slot = along(-step - ahead if way == UP else step + ahead)
        a, half = chains[chain]
        chunk = gathered.at[slot, c, half, a]
        return remote(
            chunk, chunk, ring_s.at[chain, way, step], ring_r.at[chain, way, step],
            f, up if way == UP else down,
        )

    def over_x(by, half):
        chunk = gathered.at[along(by), c, half, 1]
        return remote(chunk, chunk, slice_s.at[by % n_z], slice_r.at[by % n_z], f, across_x)

    def first_over_x(half):
        chunk = gathered.at[z, c, half, 0]
        return remote(chunk, chunk, slice_s.at[n_z], slice_r.at[n_z], f, across_x)

    def over_core(by, half, which, core):
        chunk = gathered.at[along(by), core, half]
        return remote(chunk, chunk, core_s.at[which, by % n_z], core_r.at[which, by % n_z], f, other)

    def nodes_at(distance):
        return [distance] if distance in (0, half_z) else [-distance, distance]

    def rows_of(tb, a):
        blocks = [gathered[2 * tb + n, core, half, a] for n in range(2) for core in range(2) for half in range(2)]
        return jnp.concatenate(blocks, axis=1)

    group_rows = lambda g: pl.ds(pl.multiple_of(g * GROUP, GROUP), GROUP)

    def scatter(k, off):
        return remote(
            part.at[tokens_at(off), :, group_rows(peer(k)), :], part_in.at[k - 1, tokens_at(off)],
            rs_s.at[k - 1, off % n_f], rs_r.at[k - 1, off % n_f], peer(k), m,
        )

    def products(distance):
        for d in (2 * distance, 2 * distance + 1):
            if d <= half_z:
                for by in nodes_at(d):
                    over_core(by, xh, 0, 1 - c).wait_recv()
                    over_core(by, 1 - xh, 1, 1 - c).wait_recv()
        for off in [distance] if distance in (0, half_f) else [-distance, distance]:
            tb = tokens_at(off)
            proj = dot(wt[...], rows_of(tb, 0), (1, 1)).astype(jnp.bfloat16)
            for j in range(3):
                part[tb, j] = proj[j * channels : (j + 1) * channels]
            part[tb, 3] = dot(ow[...], rows_of(tb, 1), (1, 1)).astype(jnp.bfloat16)
            for k in range(1, n_f):
                start(scatter(k, off))

    def arrived(chain, step):
        for way in (UP, DOWN):
            if step < steps[chain][way]:
                ring(chain, way, step, 1).wait_recv()
                if step + 1 < steps[chain][way]:
                    start(ring(chain, way, step + 1))

    for a in range(2):
        block = gathered.at[z, c, xh, a]
        remote(block, block, perm_s.at[a], perm_r.at[a], f, other).wait_recv()
        if a == 0:
            start(first_over_x(xh))
        for way in (UP, DOWN):
            start(ring(a, way, 0))
    start(over_x(0, xh))
    start(over_core(0, xh, 0, c))
    done = 0
    for step in range(half_z + 2):
        if step < half_z:
            for chain in range(2):
                arrived(chain, step)
            for by in nodes_at(step + 1):
                start(over_x(by, xh))
        if step == 0:
            first_over_x(1 - xh).wait_recv()
            for way in (UP, DOWN):
                start(ring(2, way, 0))
        if step >= 1:
            if step - 1 < half_z:
                arrived(2, step - 1)
            for by in nodes_at(step - 1):
                over_x(by, 1 - xh).wait_recv()
                start(over_core(by, 1 - xh, 1, c))
        if step < half_z:
            for by in nodes_at(step + 1):
                start(over_core(by, xh, 0, c))
        if step >= 2 * done + 3 and done < half_f:
            products(done)
            done += 1
    for distance in range(done, half_f + 1):
        products(distance)

    mine = group_rows(f)
    offsets = [off for d in range(half_f + 1) for off in ([d] if d in (0, half_f) else [-d, d])]
    taps = jnp.concatenate([flt[pl.ds(f, 1), :], jnp.zeros((1, BLOCK), jnp.float32)], axis=1)
    band = pltpu.roll(jnp.broadcast_to(taps, (BLOCK, 2 * BLOCK)), 0, 1, stride=1, stride_axis=0)
    band_here, band_next = band[:, :BLOCK], band[:, BLOCK:]
    for off in offsets:
        for k in range(1, n_f):
            scatter(k, off).wait_recv()

    def summed_part(j):
        total = part[:, j, mine, :].astype(jnp.float32)
        for k in range(1, n_f):
            total = total + part_in[k - 1, :, j].astype(jnp.float32)
        return total.reshape(n_f * GROUP, BLOCK)

    query, key, value = (
        summed_part(j).astype(jnp.bfloat16).astype(jnp.float32) for j in range(3)
    )
    grad_z = summed_part(3)
    nothing = jnp.zeros((GROUP, BLOCK), jnp.float32)
    product = key * value
    before = jnp.concatenate([nothing, product[:-GROUP]], axis=0)
    conv = exact(product, band_here, (1, 0)) + exact(before, band_next, (1, 0))
    grad_query = grad_z * conv
    grad_conv = grad_z * query
    after = jnp.concatenate([grad_conv[GROUP:], nothing], axis=0)
    grad_product = exact(grad_conv, band_here, (1, 1)) + exact(after, band_next, (1, 1))
    for j, grad in enumerate((grad_query, grad_product * value, grad_product * key)):
        gp[:, j, mine, :] = grad.astype(jnp.bfloat16).reshape(n_f, GROUP, BLOCK)

    tree = [d for d in (8, 7, 5, 4, 2, 6, 1, 3) if d <= half_z]
    needed = {}
    for d in tree + [0]:
        needed[d] = []
        for off in [((odd + by) // 2) % n_f for by in nodes_at(d) for odd in range(2)]:
            if off not in needed[d] and all(off not in seen for seen in needed.values()):
                needed[d].append(off)

    def share(k, off, owner):
        rows = gp.at[tokens_at(off), :, group_rows(owner), :]
        return remote(rows, rows, ag_s.at[k - 1, off], ag_r.at[k - 1, off], peer(k), m)

    for fresh in needed.values():
        for off in fresh:
            for k in range(1, n_f):
                start(share(k, off, f))

    def filter_sums():
        flip = (
            lax.broadcasted_iota(jnp.int32, (BLOCK, BLOCK), 0)
            + lax.broadcasted_iota(jnp.int32, (BLOCK, BLOCK), 1)
            == BLOCK - 1
        ).astype(jnp.float32)
        turned = exact(product, flip, (1, 0))
        corr = exact(turned, jnp.concatenate([grad_conv, after], axis=1), (0, 0))
        skewed = pltpu.roll(corr, 0, 1, stride=1, stride_axis=0)
        lags = pltpu.roll(jnp.sum(skewed, axis=0, keepdims=True), BLOCK + 1, 1)[:, :BLOCK]
        fg_all[f] = jnp.broadcast_to(lags * (1.0 / BLOCK), (8, BLOCK))

    def share_filter(k, owner):
        return remote(fg_all.at[owner], fg_all.at[owner], fg_s.at[k - 1], fg_r.at[k - 1], peer(k), m)

    def pair(off):
        chunks = pl.ds(2 * tokens_at(off), 2)
        return remote(pair_out.at[chunks], pair_in.at[chunks], pair_s.at[off], pair_r.at[off], f, other)

    def backward(off):
        for k in range(1, n_f):
            share(k, off, peer(n_f - k)).wait_recv()
        tb = tokens_at(off)
        grads = jnp.concatenate([gp[tb, j] for j in range(3)], axis=0)

        def rows_for(n, core):
            rows = pl.ds(pl.multiple_of((4 * n + 2 * core) * BLOCK, 2 * BLOCK), 2 * BLOCK)
            return dot(wn[rows, :], grads, (1, 0))

        for n in range(2):
            pair_out[2 * tb + n] = rows_for(n, 1 - c).astype(jnp.bfloat16)
        start(pair(off))
        for n in range(2):
            own[2 * tb + n] = rows_for(n, c)

    def taken(half, way, d):
        return d <= (half_z if (way == UP) == (half == 0) else half_z - 1)

    def pass_on(half, way, d):
        by = d - parent(d)
        return remote(
            ring_out.at[half, way, d - 1], ring_in.at[half, way, d - 1],
            sum_s.at[half, way, d - 1], sum_r.at[half, way, d - 1], f, node(by if way == UP else -by),
        )

    def with_children(total, half, way, at):
        for d in tree:
            if parent(d) == at and taken(half, way, d):
                pass_on(half, way, d).wait_recv()
                total = total + ring_in[half, way, d - 1].astype(jnp.float32)
        return total

    def local(slot, half):
        rows = slice(half * BLOCK, (half + 1) * BLOCK)
        return own[slot, rows, :] + pair_in[slot, rows, :].astype(jnp.float32)

    for d in tree:
        for off in needed[d]:
            backward(off)
        for off in needed[d]:
            pair(off).wait_recv()
        for way in (UP, DOWN):
            slot = along(d if way == UP else -d)
            for half in range(2):
                if taken(half, way, d):
                    ring_out[half, way, d - 1] = with_children(local(slot, half), half, way, d).astype(jnp.bfloat16)
                    start(pass_on(half, way, d))
        if d == 2:
            filter_sums()
            for k in range(1, n_f):
                start(share_filter(k, f))
    for off in needed[0]:
        backward(off)
        pair(off).wait_recv()

    for half in range(2):
        total = local(z, half)
        for way in (UP, DOWN):
            total = with_children(total, half, way, 0)
        last_out[half] = total.astype(jnp.bfloat16)
        start(remote(
            last_out.at[half], last_in.at[xh], last_s.at[half], last_r.at[xh], from_f, from_m(half)
        ))
    for k in range(1, n_f):
        share_filter(k, peer(n_f - k)).wait_recv()
    filter_grad[...] = jnp.concatenate([fg_all[g, 0:1, :] for g in range(n_f)], axis=0)
    for copy in sent[:-2]:
        copy.wait_send()
    for x in range(2):
        remote(last_out.at[x], last_in.at[x], last_s.at[x], last_r.at[x], to_f, to_m(x)).wait_recv()
    summed = last_in[0].astype(jnp.float32) + last_in[1].astype(jnp.float32)
    input_grad[...] = summed.T.astype(jnp.bfloat16)
    for copy in sent[-2:]:
        copy.wait_send()


def on_device(n_f, n_z, tokens, in_values, in_scales, filters, out_weight, cotangent):
    channels = in_values.shape[2]
    features = PIECES * BLOCK
    bf16, f32 = jnp.bfloat16, jnp.float32
    dma = pltpu.SemaphoreType.DMA
    values, scales = in_values.transpose(1, 0, 2), in_scales.transpose(1, 0, 2)
    return pl.pallas_call(
        functools.partial(kernel, n_f, n_z),
        out_shape=(
            jax.ShapeDtypeStruct((BLOCK, BLOCK), bf16),
            jax.ShapeDtypeStruct((n_f, BLOCK), f32),
        ),
        in_specs=[pl.BlockSpec(memory_space=pl.ANY)] * 6,
        out_specs=(pl.BlockSpec(memory_space=pltpu.VMEM),) * 2,
        scratch_shapes=[
            pltpu.VMEM(values.shape, bf16),
            pltpu.VMEM(scales.shape, bf16),
            pltpu.VMEM(filters.shape, f32),
            pltpu.VMEM(out_weight.shape, bf16),
            pltpu.VMEM((n_z, 2, 2, 2, BLOCK, BLOCK), bf16),
            pltpu.VMEM((3 * channels, features), bf16),
            pltpu.VMEM((features, 3 * channels), bf16),
            pltpu.VMEM((channels, features), bf16),
            pltpu.VMEM((n_f, 4, channels, BLOCK), bf16),
            pltpu.VMEM((n_f - 1, n_f, 4, GROUP, BLOCK), bf16),
            pltpu.VMEM((n_f, 3, channels, BLOCK), bf16),
            pltpu.VMEM((n_f, 8, BLOCK), f32),
            pltpu.VMEM((n_z, 2 * BLOCK, BLOCK), f32),
            pltpu.VMEM((n_z, 2 * BLOCK, BLOCK), bf16),
            pltpu.VMEM((n_z, 2 * BLOCK, BLOCK), bf16),
            pltpu.VMEM((2, 2, n_z // 2, BLOCK, BLOCK), bf16),
            pltpu.VMEM((2, 2, n_z // 2, BLOCK, BLOCK), bf16),
            pltpu.VMEM((2, BLOCK, BLOCK), bf16),
            pltpu.VMEM((2, BLOCK, BLOCK), bf16),
            dma((4,)),
            dma((2,)), dma((2,)),
            dma((3, 2, n_z // 2)), dma((3, 2, n_z // 2)),
            dma((n_z + 1,)), dma((n_z + 1,)),
            dma((2, n_z)), dma((2, n_z)),
            dma((n_f - 1, n_f)), dma((n_f - 1, n_f)),
            dma((n_f - 1, n_f)), dma((n_f - 1, n_f)),
            dma((n_f - 1,)), dma((n_f - 1,)),
            dma((n_f,)), dma((n_f,)),
            dma((2, 2, n_z // 2)), dma((2, 2, n_z // 2)),
            dma((2,)), dma((2,)),
        ],
        compiler_params=pltpu.CompilerParams(
            collective_id=0, has_side_effects=True, vmem_limit_bytes=56 << 20
        ),
        name="hyena",
    )(tokens, cotangent, values, scales, filters, out_weight)


def solution(mesh):
    placed = (
        P("fsdp", "tensor"),
        P("fsdp", None, "tensor"),
        P("fsdp", None, "tensor"),
        P("tensor", None),
        P("tensor", "fsdp"),
        P("fsdp", "tensor"),
    )
    return jax.shard_map(
        functools.partial(on_device, mesh.shape["fsdp"], mesh.shape["tensor"] // 4),
        mesh=mesh,
        in_specs=placed,
        out_specs=(P("fsdp", "tensor"), P("tensor", None)),
        check_vma=False,
    )
```
